256 devices in a mesh: ctx: 32 (over z, x), tp: 8 (over y, core).
Axes of the slice: x: 4, y: 4, z: 8, core: 2. Of those that a mesh axis runs over, the one named last changes fastest.
Arguments:
- tokens: bfloat16 [24576, 4096], P('ctx'), may hold values from -6 to 6
- qkv_weight: bfloat16 [3, 4096, 4096], P(None, 'ctx', 'tp'), may hold values from -0.09375 to 0.09375
- short_filter: float32 [3, 7, 4096], P(None, None, 'tp'), may hold values from -2.4 to 2.4
- long_filter: float32 [256, 128], P('tp'), may hold values from -0.9 to 0.9
- decay_rate: float32 [256], P('tp'), may hold values from 0.004 to 0.2
- skip_gain: float32 [4096], P('tp'), may hold values from -3 to 3
- out_weight: bfloat16 [4096, 4096], P('tp', 'ctx'), may hold values from -0.09375 to 0.09375
Outputs:
- block_out: bfloat16 [24576, 4096], P(('ctx', 'tp'))
The draws below stay inside these ranges and needn't reach their ends.
All inputs are finite; a program needn't handle non-finite values.
Results may differ from the reference program's by a relative error of at most 0.008.
Values may be sent and summed in bfloat16 or wider, within the bound.
A program may use at most 64 MiB of HBM per device.

```python
import math
import jax
import jax.numpy as jnp
from jax import lax

D = 4096
C = 4096
G = 16
TAPS = 128
SHORT = 7
TOKENS = 24576
GROUPS = 256


def steps_of(rng, dims, split, low, top_value):
    level, own = 1.0, jax.random.fold_in(rng, 6)
    for dim, shards_of in split:
        heights = jnp.exp(jax.random.uniform(jax.random.fold_in(own, dim), (shards_of,), jnp.float32, low / len(split), top_value / len(split)))
        level = level * jnp.repeat(heights, dims[dim] // shards_of).reshape([-1 if axis == dim else 1 for axis in range(len(dims))])
    return level


def bell_draw(stream_key, shape, scale, reach, split=(), kind=jnp.bfloat16):
    factor_of = steps_of(stream_key, shape, split, -0.22, 0.18) if split else 1.0
    values = jax.random.normal(stream_key, shape, jnp.float32) * scale * factor_of
    return jnp.minimum(jnp.maximum(values, -reach), reach).astype(kind)


def setup_inputs(seed: int = 0) -> dict:
    arg_keys = jax.random.split(jax.random.key(seed), 8)
    tokens = bell_draw(arg_keys[0], (TOKENS, D), 1.0, 6.0, ((0, 32),))
    qkv_weight = bell_draw(arg_keys[1], (3, D, C), D ** -0.5, 0.09375, ((1, 32), (2, 8)))
    short_filter = bell_draw(arg_keys[2], (3, SHORT, C), 0.4, 2.4, ((2, 8),), jnp.float32)
    long_filter = bell_draw(arg_keys[3], (GROUPS, TAPS), 0.15, 0.9, ((0, 8),), jnp.float32)
    decay_rate = jnp.clip(jnp.exp(math.log(0.2) - 3.912023 * jax.random.uniform(arg_keys[4], (GROUPS,), jnp.float32) ** steps_of(arg_keys[4], (GROUPS,), ((0, 8),), -0.2, 0.2)), 0.004, 0.2)
    skip_gain = bell_draw(arg_keys[5], (C,), 0.5, 3.0, ((0, 8),), jnp.float32)
    out_weight = bell_draw(arg_keys[6], (C, D), C ** -0.5, 0.09375, ((0, 8), (1, 32)))
    return {"tokens": tokens, "qkv_weight": qkv_weight, "short_filter": short_filter, "long_filter": long_filter, "decay_rate": decay_rate, "skip_gain": skip_gain, "out_weight": out_weight}


def reference(tokens, qkv_weight, short_filter, long_filter, decay_rate, skip_gain, out_weight):
    projected = jnp.stack([jnp.dot(tokens, qkv_weight[index], preferred_element_type=jnp.float32) for index in range(3)])
    qkv = projected.astype(jnp.bfloat16)
    padded = jnp.pad(qkv, ((0, 0), (SHORT - 1, 0), (0, 0)))
    features = short_filter[:, 0, None, :] * padded[:, SHORT - 1:, :]
    for offset in range(1, SHORT):
        start = SHORT - 1 - offset
        features = features + short_filter[:, offset, None, :] * padded[:, start:start + TOKENS, :]
    gated = (features[1] * features[2]).astype(jnp.bfloat16)
    tap_index = jnp.arange(TAPS, dtype=jnp.float32)
    filters = (long_filter * jnp.exp(-decay_rate[:, None] * tap_index[None, :])).astype(jnp.bfloat16)
    per_tap = jnp.repeat(filters, G, axis=0).astype(jnp.float32).T
    gated_wide = gated.astype(jnp.float32)
    gated_pad = jnp.pad(gated_wide, ((TAPS - 1, 0), (0, 0)))

    def add_tap(step, total):
        step_int = jnp.asarray(step).astype(jnp.int32)
        weights = lax.dynamic_index_in_dim(per_tap, step_int, 0, keepdims=False)
        window = lax.dynamic_slice_in_dim(gated_pad, (TAPS - 1 - step_int).astype(jnp.int32), TOKENS, 0)
        return total + weights[None, :] * window

    filtered = lax.fori_loop(0, TAPS, add_tap, jnp.zeros((TOKENS, C), jnp.float32))
    mixed = (features[0] * (filtered + skip_gain[None, :] * gated_wide)).astype(jnp.bfloat16)
    return jnp.dot(mixed, out_weight, preferred_element_type=jnp.float32).astype(jnp.bfloat16)
```

```python
import jax
import jax.numpy as jnp
from jax import lax
from jax.sharding import PartitionSpec as P


def short_conv(extended, short_filter):
    span = short_filter.shape[1]
    length = extended.shape[2] - (span - 1)
    result = short_filter[:, 0, :, None] * extended[:, :, span - 1 :]
    for offset in range(1, span):
        start = span - 1 - offset
        result = result + short_filter[:, offset, :, None] * extended[:, :, start : start + length]
    return result


def banded(filters):
    tap_count = filters.shape[1]
    row_index = jnp.arange(tap_count)[:, None]
    col_index = jnp.arange(tap_count)[None, :]
    distance = (row_index - col_index) % tap_count
    picker = (distance[None, :, :] == jnp.arange(tap_count)[:, None, None]).astype(jnp.bfloat16)
    full_band = jnp.einsum("gk,kij->gij", filters, picker, preferred_element_type=jnp.float32)
    lower_part = row_index >= col_index
    lower_band = jnp.where(lower_part[None], full_band, 0.0).astype(jnp.bfloat16)
    upper_band = jnp.where(lower_part[None], 0.0, full_band).astype(jnp.bfloat16)
    return (lower_band, upper_band)


def long_mix(features, gated, previous, filters, gain):
    channel_count, length = gated.shape
    tap_count = filters.shape[1]
    group_count = filters.shape[0]
    extended = jnp.concatenate([previous, gated], axis=1)
    blocks = extended.reshape(
        group_count, channel_count // group_count, length // tap_count + 1, tap_count
    )
    lower_band, upper_band = banded(filters)
    current = jnp.einsum(
        "gij,gcbj->gcbi", lower_band, blocks[:, :, 1:], preferred_element_type=jnp.float32
    )
    current = current + jnp.einsum(
        "gij,gcbj->gcbi", upper_band, blocks[:, :, :-1], preferred_element_type=jnp.float32
    )
    filtered = current.reshape(channel_count, length)
    return (features[0] * (filtered + gain[:, None] * gated.astype(jnp.float32))).astype(
        jnp.bfloat16
    )


def per_device(tokens, qkv_weight, short_filter, long_filter, decay_rate, skip_gain, out_weight):
    tap_count = long_filter.shape[1]
    span = short_filter.shape[1]
    projected = jnp.einsum(
        "tr,src->sct",
        tokens,
        lax.all_gather(qkv_weight, "ctx", axis=1, tiled=True),
        preferred_element_type=jnp.float32,
    )
    qkv = projected.astype(jnp.bfloat16)
    tap_index = jnp.arange(tap_count, dtype=jnp.float32)
    filters = (long_filter * jnp.exp(-decay_rate[:, None] * tap_index[None, :])).astype(
        jnp.bfloat16
    )
    halo = tap_count + span - 1
    count = lax.axis_size("ctx")
    tail = lax.ppermute(
        qkv[:, :, qkv.shape[2] - halo :], "ctx", [(i, i + 1) for i in range(count - 1)]
    )
    features = short_conv(jnp.concatenate([tail, qkv], axis=2), short_filter)
    gated = (features[1] * features[2]).astype(jnp.bfloat16)
    mixed = long_mix(
        features[:, :, tap_count:],
        gated[:, tap_count:],
        gated[:, :tap_count],
        filters,
        skip_gain,
    )
    out_rows = lax.all_gather(out_weight, "ctx", axis=1, tiled=True)
    summed = lax.psum_scatter(
        lax.dot_general(
            mixed, out_rows, (((0,), (0,)), ((), ())), preferred_element_type=jnp.float32
        ).astype(jnp.bfloat16),
        "tp",
        scatter_dimension=0,
        tiled=True,
    )
    return summed.astype(jnp.bfloat16)


def solution(mesh):
    in_specs = (
        P("ctx", None),
        P(None, "ctx", "tp"),
        P(None, None, "tp"),
        P("tp", None),
        P("tp"),
        P("tp"),
        P("tp", "ctx"),
    )
    out_specs = P(("ctx", "tp"), None)
    return jax.shard_map(
        per_device, mesh=mesh, in_specs=in_specs, out_specs=out_specs, check_vma=False
    )
```

```python
import jax
import jax.numpy as jnp
from jax import lax
from jax.experimental import pallas as pl
from jax.experimental.pallas import tpu as pltpu
from jax.sharding import PartitionSpec as P

MESH = pl.DeviceIdType.MESH
NZ, NX, NY = 8, 4, 4
ROUNDS = (0, 1, 7, 2, 6, 3, 5, 4)
CHUNKS = ((0, (0,)), (1, (1, 7)), (7, ()), (2, (2, 6)), (6, ()), (3, (3, 5)), (5, ()), (4, (4,)))


class Gather:
    def __init__(self, place, slot, send_sem, recv_sem):
        self.z, self.x, self.step = place
        self.slot, self.send_sem, self.recv_sem = slot, send_sem, recv_sem
        self.sent = []

    def source(self, dz, dx):
        z = lax.rem(self.z - self.step * dz + NZ, NZ)
        x = lax.rem(self.x - self.step * dx + NX, NX)
        return z * NX + x

    def copy(self, part, dz, dx, axis, way):
        ref = self.slot(part, self.source(dz, dx))
        z, x = self.z, self.x
        if axis == "z":
            z, dz = lax.rem(z + way * self.step + NZ, NZ), (dz + way) % NZ
        else:
            x, dx = lax.rem(x + way * self.step + NX, NX), (dx + way) % NX
        return pltpu.make_async_remote_copy(
            src_ref=ref,
            dst_ref=ref,
            send_sem=self.send_sem.at[part, dz, dx],
            recv_sem=self.recv_sem.at[part, dz, dx],
            device_id={"ctx": z * NX + x},
            device_id_type=MESH,
        )

    def send(self, *args):
        copy = self.copy(*args)
        copy.start()
        self.sent.append(copy)

    def wait(self, part, dz, dx):
        if (dz, dx) != (0, 0):
            ref = self.slot(part, self.source(dz, dx))
            pltpu.make_async_remote_copy(
                src_ref=ref,
                dst_ref=ref,
                send_sem=self.send_sem.at[part, dz, dx],
                recv_sem=self.recv_sem.at[part, dz, dx],
                device_id={"ctx": lax.rem(self.z + 1, NZ) * NX + self.x},
                device_id_type=MESH,
            ).wait_recv()

    def along_z(self, part, dz, dx):
        if dz <= NZ // 2 - 1:
            self.send(part, dz, dx, "z", 1)
        if dz == 0 or dz > NZ // 2 + 1:
            self.send(part, dz, dx, "z", -1)

    def along_x(self, part, dz, dx):
        if dx <= NX // 2 - 1:
            self.send(part, dz, dx, "x", 1)
        if dx == 0 or dx > NX // 2 + 1:
            self.send(part, dz, dx, "x", -1)

    def arrive0(self, dz, dx):
        self.wait(0, dz, dx)
        if dx == 0:
            self.along_z(0, dz, dx)
        self.along_x(0, dz, dx)

    def arrive1(self, dz, dx):
        self.wait(1, dz, dx)
        if dz == 0:
            self.along_x(1, dz, dx)
        self.along_z(1, dz, dx)

    def service(self, index):
        dz = ROUNDS[index]
        self.arrive0(dz, 0)
        for dx in (0, 1, 3, 2):
            self.arrive1(dz, dx)
        self.arrive0(dz, 1)

    def complete(self, dz):
        self.arrive0(dz, 3)
        self.arrive0(dz, 2)

    def finish(self):
        for copy in self.sent:
            copy.wait_send()


def kernel(
    tokens_hbm, qkv_hbm, short_ref, long_ref, decay_ref, gain_ref, out_hbm,
    result_ref,
    tok, wq, wo, acc, quer, gat, band, mix, mixp, own,
    cs_send, cs_recv, fs, fr, ms, mr, js, jr, tail_send, tail_recv, halo,
    local_sem, wq_ss, wq_rs, wo_ss, wo_rs, cs_ss, cs_rs, y_ss, y_rs, halo_ss, halo_rs,
):
    ctx, tp = lax.axis_index("ctx"), lax.axis_index("tp")
    z, x = lax.div(ctx, NX), lax.rem(ctx, NX)
    y, core = lax.div(tp, 2), lax.rem(tp, 2)
    step = 1 - 2 * core
    tcount, depth = tok.shape
    share = qkv_hbm.shape[1]
    width = qkv_hbm.shape[2]
    count = NZ * NX
    block = tcount // (2 * NY)
    half = NY * block

    local = [pltpu.make_async_copy(qkv_hbm.at[i], wq.at[pl.ds(pl.multiple_of(ctx * share, share), share), pl.ds(i * width, width)], local_sem.at[i]) for i in range(3)]
    local.append(pltpu.make_async_copy(out_hbm, wo.at[ctx], local_sem.at[3]))
    local.append(pltpu.make_async_copy(tokens_hbm, tok, local_sem.at[4]))
    for copy in local:
        copy.start()

    after = {"ctx": lax.rem(ctx + 1, count)}
    partner = {"tp": tp + step}
    y_up = {"tp": lax.rem(y + step + NY, NY) * 2 + core}
    y_down = {"tp": lax.rem(y - step + NY, NY) * 2 + core}
    barrier = pltpu.get_barrier_semaphore()
    neighbours = [
        {"ctx": lax.rem(z + 1, NZ) * NX + x},
        {"ctx": lax.rem(z + NZ - 1, NZ) * NX + x},
        {"ctx": z * NX + lax.rem(x + 1, NX)},
        {"ctx": z * NX + lax.rem(x + NX - 1, NX)},
        after,
        {"ctx": lax.rem(ctx + count - 1, count)},
        partner,
        y_up,
        y_down,
    ]
    for device in neighbours:
        pl.semaphore_signal(barrier, inc=1, device_id=device, device_id_type=MESH)
    pl.semaphore_wait(barrier, len(neighbours))

    cut = 7 * 128
    ocut = 304

    def wq_slot(part, source):
        rows = pl.ds(pl.multiple_of(source * share, share), share)
        return wq.at[rows, pl.ds(0, cut)] if part == 0 else wq.at[rows, pl.ds(cut, 3 * width - cut)]

    def wo_slot(part, source):
        return wo.at[source, pl.ds(0, ocut), :] if part == 0 else wo.at[source, pl.ds(ocut, width - ocut), :]

    place = (z, x, step)
    wg = Gather(place, wq_slot, wq_ss, wq_rs)
    og = Gather(place, wo_slot, wo_ss, wo_rs)

    for copy in local[:3]:
        copy.wait()
    wg.service(0)
    for copy in local[3:]:
        copy.wait()

    taps = long_ref.shape[1]
    lane = lax.broadcasted_iota(jnp.int32, (1, taps), 1).astype(jnp.float32)
    row_id = lax.broadcasted_iota(jnp.int32, (taps, taps), 0)
    col_id = lax.broadcasted_iota(jnp.int32, (taps, taps), 1)

    def build(group, carry):
        filt = long_ref[pl.ds(group, 1), :] * jnp.exp(-decay_ref[pl.ds(group, 1), :] * lane)
        ring = pltpu.roll(jnp.broadcast_to(filt, (taps, taps)), 0, 1, stride=1, stride_axis=0).T
        rows = pl.ds(pl.multiple_of(group * taps, taps), taps)
        band[rows, 0:taps] = jnp.where(col_id > row_id, ring, 0.0).astype(jnp.bfloat16)
        band[rows, taps : 2 * taps] = jnp.where(col_id <= row_id, ring, 0.0).astype(jnp.bfloat16)
        return carry

    lax.fori_loop(0, long_ref.shape[0], build, 0)

    lead = 8
    span = NX * share
    tile = 256

    def project(dz, first, last):
        source = lax.rem(z - step * dz + NZ, NZ)
        rows = pl.ds(pl.multiple_of(source * span, span), span)

        def one(n, carry):
            cols = pl.ds(pl.multiple_of(n * tile, tile), tile)
            part = jnp.dot(tok[:, rows], wq[rows, cols], preferred_element_type=jnp.float32)
            if not first:
                part = part + acc[lead:, cols]
            if last:
                part = part.astype(jnp.bfloat16).astype(jnp.float32)
            acc[lead:, cols] = part
            return carry

        lax.fori_loop(0, 3 * width // tile, one, 0)

    for index in range(1, NZ):
        wg.service(index)
        dz = ROUNDS[index - 1]
        wg.complete(dz)
        project(dz, index == 1, False)
    og.service(0)
    wg.complete(ROUNDS[-1])
    project(ROUNDS[-1], False, True)

    def remote(src, dst, ss, rs, device):
        return pltpu.make_async_remote_copy(src_ref=src, dst_ref=dst, send_sem=ss, recv_sem=rs, device_id=device, device_id_type=MESH)

    tail_send[...] = acc[lead + tcount - 16 :, :].astype(jnp.bfloat16)
    tail_copy = remote(tail_send, tail_recv, halo_ss.at[0], halo_rs.at[0], after)
    tail_copy.start()

    reach = short_ref.shape[1]
    lanes = 128

    def feature(s, r, c):
        cols = pl.ds(pl.multiple_of(s * width + c * lanes, lanes), lanes)
        own_cols = pl.ds(pl.multiple_of(c * lanes, lanes), lanes)
        window = acc[pl.ds(pl.multiple_of(r * taps, taps), taps + lead), cols]
        total = window[lead:] * short_ref[s, 0:1, own_cols]
        for j in range(1, reach):
            total = total + pltpu.roll(window, j, 0)[lead:] * short_ref[s, j : j + 1, own_cols]
        return total

    def features(r, c):
        rows = pl.ds(pl.multiple_of(r * taps, taps), taps)
        cols = pl.ds(pl.multiple_of(c * lanes, lanes), lanes)
        gat[pl.ds(pl.multiple_of(r * taps + taps, taps), taps), cols] = (feature(1, r, c) * feature(2, r, c)).astype(jnp.bfloat16)
        quer[rows, cols] = feature(0, r, c)

    tiles = width // lanes
    blocks = tcount // taps
    lax.fori_loop(0, tiles, lambda c, k: (features(blocks - 1, c), k)[1], 0)
    halo_copy = remote(gat.at[pl.ds(tcount, taps), :], halo, halo_ss.at[1], halo_rs.at[1], after)
    halo_copy.start()
    og.service(1)

    def later(i, carry):
        features(lax.div(i, tiles) + 1, lax.rem(i, tiles))
        return carry

    lax.fori_loop(0, (blocks - 2) * tiles, later, 0)
    tail_copy.wait_recv()
    acc[0:lead, :] = jnp.where(ctx > 0, tail_recv[...].astype(jnp.float32)[16 - lead :, :], 0.0)
    lax.fori_loop(0, tiles, lambda c, k: (features(0, c), k)[1], 0)
    og.service(2)
    og.complete(0)
    halo_copy.wait_recv()
    gat[0:taps, :] = jnp.where(ctx > 0, halo[...].astype(jnp.float32), 0.0).astype(jnp.bfloat16)

    group_of = lax.broadcasted_iota(jnp.int32, (taps, 2 * lanes), 1) % lanes // 16
    per_tile = lanes // 16

    def convolve(i, carry):
        p, c = lax.div(i, tiles), lax.rem(i, tiles)
        cols = pl.ds(pl.multiple_of(c * lanes, lanes), lanes)
        base = p * 2 * taps

        def at(offset, size):
            return pl.ds(pl.multiple_of(base + offset, taps), size)

        right = jnp.concatenate([gat[at(0, 2 * taps), cols], gat[at(taps, 2 * taps), cols]], axis=1)
        left = band[pl.ds(pl.multiple_of(c * per_tile * taps, taps), per_tile * taps), :]
        every = jnp.dot(left, right, preferred_element_type=jnp.float32)
        total = every[0:taps]
        for g in range(1, per_tile):
            total = jnp.where(group_of >= g, every[g * taps : (g + 1) * taps], total)
        gain = gain_ref[0:1, cols]
        for h in range(2):
            gated = gat[at((h + 1) * taps, taps), cols].astype(jnp.float32)
            rows = at(h * taps, taps)
            mix[rows, cols] = (quer[rows, cols] * (total[:, h * lanes : (h + 1) * lanes] + gain * gated)).astype(jnp.bfloat16)
        return carry

    pairs = blocks // 2
    lax.fori_loop(0, tiles, convolve, 0)
    og.service(3)
    og.complete(ROUNDS[1])
    og.complete(ROUNDS[2])
    lax.fori_loop(tiles, pairs * tiles, convolve, 0)

    for side in range(2):
        ahead = -step if side == 0 else step
        to_core = 1 - core if side == 0 else core
        for j in range(NY):
            to = lax.rem(y + ahead * j + NY, NY) * 2 + to_core
            mixp[side * half + j * block : side * half + (j + 1) * block, :] = mix[pl.ds(pl.multiple_of(to * block, 16), block), :]

    def stage0(k):
        offset, needs = CHUNKS[k]
        zsrc = lax.rem(z + offset, NZ)
        for i in range(NX // 2):
            right = jnp.concatenate([wo[zsrc * NX + 2 * i], wo[zsrc * NX + 2 * i + 1]], axis=1)
            cols = slice(2 * i * share, 2 * (i + 1) * share)
            cs_send[k, :, cols] = jnp.dot(mixp[0:half, :], right, preferred_element_type=jnp.float32).astype(jnp.bfloat16)
        copy = remote(cs_send.at[k], cs_recv.at[k], cs_ss.at[k], cs_rs.at[k], partner)
        copy.start()
        for i in range(NX // 2):
            right = jnp.concatenate([wo[zsrc * NX + 2 * i], wo[zsrc * NX + 2 * i + 1]], axis=1)
            cols = slice(2 * i * share, 2 * (i + 1) * share)
            own[k % 4, :, cols] = jnp.dot(mixp[half:, :], right, preferred_element_type=jnp.float32)
        return copy

    def rows_of(j):
        return slice(j * block, (j + 1) * block)

    def stage1(k):
        cs[k].wait_recv()
        slot = k % 4
        fs[k] = (own[slot, rows_of(2)] + cs_recv[k, rows_of(2)].astype(jnp.float32)).astype(jnp.bfloat16)
        first = remote(fs.at[k], fr.at[k], y_ss.at[0, k], y_rs.at[0, k], y_up)
        first.start()
        ms[k] = (own[slot, rows_of(3)] + cs_recv[k, rows_of(3)].astype(jnp.float32)).astype(jnp.bfloat16)
        minor = remote(ms.at[k], mr.at[k], y_ss.at[1, k], y_rs.at[1, k], y_down)
        minor.start()
        own[slot, 0 : 2 * block] = own[slot, 0 : 2 * block] + cs_recv[k, 0 : 2 * block].astype(jnp.float32)
        return first, minor

    def stage2(k):
        ys[k][0].wait_recv()
        js[k] = (own[k % 4, rows_of(1)] + fr[k].astype(jnp.float32)).astype(jnp.bfloat16)
        joined = remote(js.at[k], jr.at[k], y_ss.at[2, k], y_rs.at[2, k], y_up)
        joined.start()
        return joined

    def stage3(k):
        ys[k][1].wait_recv()
        jn[k].wait_recv()
        zsrc = lax.rem(z + CHUNKS[k][0], NZ)
        total = own[k % 4, rows_of(0)] + mr[k].astype(jnp.float32) + jr[k].astype(jnp.float32)
        result_ref[:, pl.ds(pl.multiple_of(zsrc * span, span), span)] = total.astype(jnp.bfloat16)

    cs, ys, jn = {}, {}, {}
    done = {0, ROUNDS[1], ROUNDS[2]}
    served = 3
    for k in range(NZ + 3):
        if k < NZ:
            for dz in CHUNKS[k][1]:
                while dz not in done:
                    if served < NZ - 1:
                        served += 1
                        og.service(served)
                    if dz == ROUNDS[served] or dz in ROUNDS[:served]:
                        og.complete(dz)
                        done.add(dz)
            cs[k] = stage0(k)
        if 1 <= k < NZ + 1:
            ys[k - 1] = stage1(k - 1)
        if 2 <= k < NZ + 2:
            jn[k - 2] = stage2(k - 2)
        if k >= 3:
            stage3(k - 3)

    wg.finish()
    og.finish()
    tail_copy.wait_send()
    halo_copy.wait_send()
    for k in range(NZ):
        cs[k].wait_send()
        ys[k][0].wait_send()
        ys[k][1].wait_send()
        jn[k].wait_send()


def per_device(tokens, qkv_weight, short_filter, long_filter, decay_rate, skip_gain, out_weight):
    tcount, depth = tokens.shape
    _, share, width = qkv_weight.shape
    taps = long_filter.shape[1]
    groups = long_filter.shape[0]
    span = NX * share
    block = tcount // (2 * NY)
    half = NY * block
    bf, f32 = jnp.bfloat16, jnp.float32
    dma = pltpu.SemaphoreType.DMA
    any_spec = pl.BlockSpec(memory_space=pl.ANY)
    vmem = pl.BlockSpec(memory_space=pltpu.VMEM)
    small = (NZ, block, span)
    return pl.pallas_call(
        kernel,
        out_shape=jax.ShapeDtypeStruct((block, depth), bf),
        in_specs=[any_spec, any_spec, vmem, vmem, vmem, vmem, any_spec],
        out_specs=vmem,
        scratch_shapes=[
            pltpu.VMEM((tcount, depth), bf),
            pltpu.VMEM((depth, 3 * width), bf),
            pltpu.VMEM((NZ * NX, width, share), bf),
            pltpu.VMEM((8 + tcount, 3 * width), f32),
            pltpu.VMEM((tcount, width), f32),
            pltpu.VMEM((taps + tcount, width), bf),
            pltpu.VMEM((groups * taps, 2 * taps), bf),
            pltpu.VMEM((tcount, width), bf),
            pltpu.VMEM((tcount, width), bf),
            pltpu.VMEM((4, half, span), f32),
            pltpu.VMEM((NZ, half, span), bf),
            pltpu.VMEM((NZ, half, span), bf),
            *[pltpu.VMEM(small, bf) for _ in range(6)],
            pltpu.VMEM((16, 3 * width), bf),
            pltpu.VMEM((16, 3 * width), bf),
            pltpu.VMEM((taps, width), bf),
            dma((5,)),
            dma((2, NZ, NX)),
            dma((2, NZ, NX)),
            dma((2, NZ, NX)),
            dma((2, NZ, NX)),
            dma((NZ,)),
            dma((NZ,)),
            dma((3, NZ)),
            dma((3, NZ)),
            dma((2,)),
            dma((2,)),
        ],
        compiler_params=pltpu.CompilerParams(
            collective_id=0, has_side_effects=True, vmem_limit_bytes=67043328
        ),
    )(
        tokens,
        qkv_weight,
        short_filter,
        long_filter,
        decay_rate[:, None],
        skip_gain[None, :],
        out_weight,
    )


def solution(mesh):
    in_specs = (
        P("ctx", None),
        P(None, "ctx", "tp"),
        P(None, None, "tp"),
        P("tp", None),
        P("tp"),
        P("tp"),
        P("tp", "ctx"),
    )
    out_specs = P(("ctx", "tp"), None)
    return jax.shard_map(
        per_device, mesh=mesh, in_specs=in_specs, out_specs=out_specs, check_vma=False
    )
```

```python
import jax
import jax.numpy as jnp
from jax import lax
from jax.experimental import pallas as pl
from jax.experimental.pallas import tpu as pltpu
from jax.sharding import PartitionSpec as P

MESH = pl.DeviceIdType.MESH
NZ, NX, NY = 8, 4, 4
ORDER = (
    36, 60, 1, 3, 4, 28, 33, 35, 2, 40, 56, 5, 7, 8, 24, 37, 61, 29, 31, 39, 63, 34, 11, 44, 52,
    6, 27, 12, 20, 9, 25, 41, 57, 43, 59, 15, 30, 38, 62, 13, 23, 48, 53, 21, 10, 55, 16, 26,
    58, 45, 14, 47, 19, 42, 22, 54, 49, 17, 64, 51, 46, 124, 100, 67, 92, 99, 68, 18, 65, 120,
    50, 97, 104, 88, 93, 95, 103, 127, 69, 71, 72, 116, 66, 101, 125, 98, 108, 91, 89, 84, 107,
    75, 123, 94, 76, 70, 121, 105, 73, 126, 102, 87, 90, 119, 112, 117, 111, 79, 85, 77, 122,
    80, 74, 109, 106, 115, 86, 118, 78, 113, 83, 110, 81, 114, 82,
)
CHUNKS = ((0, (0,)), (1, (1, 7)), (7, (1, 7)), (2, (2, 6)), (6, (2, 6)), (3, (3, 5)), (5, (3, 5)), (4, (4,)))


class Gather:
    def __init__(self, place, slot, send_sem, recv_sem):
        self.z, self.x, self.step = place
        self.slot, self.send_sem, self.recv_sem = slot, send_sem, recv_sem
        self.sent = []

    def source(self, dz, dx):
        z = lax.rem(self.z - self.step * dz + NZ, NZ)
        x = lax.rem(self.x - self.step * dx + NX, NX)
        return z * NX + x

    def copy(self, part, dz, dx, axis, way):
        ref = self.slot(part, self.source(dz, dx))
        z, x = self.z, self.x
        if axis == "z":
            z, dz = lax.rem(z + way * self.step + NZ, NZ), (dz + way) % NZ
        else:
            x, dx = lax.rem(x + way * self.step + NX, NX), (dx + way) % NX
        return pltpu.make_async_remote_copy(
            src_ref=ref,
            dst_ref=ref,
            send_sem=self.send_sem.at[part, dz, dx],
            recv_sem=self.recv_sem.at[part, dz, dx],
            device_id={"ctx": z * NX + x},
            device_id_type=MESH,
        )

    def send(self, *args):
        copy = self.copy(*args)
        copy.start()
        self.sent.append(copy)

    def wait(self, part, dz, dx):
        if (dz, dx) != (0, 0):
            ref = self.slot(part, self.source(dz, dx))
            pltpu.make_async_remote_copy(
                src_ref=ref,
                dst_ref=ref,
                send_sem=self.send_sem.at[part, dz, dx],
                recv_sem=self.recv_sem.at[part, dz, dx],
                device_id={"ctx": lax.rem(self.z + 1, NZ) * NX + self.x},
                device_id_type=MESH,
            ).wait_recv()

    def targets(self, part, dz, dx):
        along_z = [w for w, go in ((1, dz < NZ // 2), (-1, dz == 0 or dz > NZ // 2 + 1)) if go]
        along_x = [w for w, go in ((1, dx < NX // 2), (-1, dx == 0 or dx > NX // 2 + 1)) if go]
        if part == 0:
            first = [(part, dz, dx, "x", w) for w in along_x]
            return first, [(part, dz, dx, "z", w) for w in along_z] if dx == 0 else []
        first = [(part, dz, dx, "z", w) for w in along_z]
        return first, [(part, dz, dx, "x", w) for w in along_x] if dz == 0 else []

    def begin(self):
        both = [self.targets(part, 0, 0) for part in range(2)]
        for target in [t for i in range(2) for pair in both for t in pair[i]]:
            self.send(*target)

    def arrive(self, part, dz, dx):
        self.wait(part, dz, dx)
        first, second = self.targets(part, dz, dx)
        for target in first + second:
            self.send(*target)

    def finish(self):
        for copy in self.sent:
            copy.wait_send()


def kernel(
    tokens_hbm, qkv_hbm, short_ref, long_ref, decay_ref, gain_ref, out_hbm,
    result_ref,
    tok, wq, wo, acc, quer, gat, band, mix, mixp, own,
    cs_send, cs_recv, fs, fr, ms, mr, js, jr, tail_send, tail_recv, halo,
    local_sem, wq_ss, wq_rs, wo_ss, wo_rs, cs_ss, cs_rs, y_ss, y_rs, halo_ss, halo_rs,
):
    ctx, tp = lax.axis_index("ctx"), lax.axis_index("tp")
    z, x = lax.div(ctx, NX), lax.rem(ctx, NX)
    y, core = lax.div(tp, 2), lax.rem(tp, 2)
    step = 1 - 2 * core
    tcount, depth = tok.shape
    share = qkv_hbm.shape[1]
    width = qkv_hbm.shape[2]
    count = NZ * NX
    block = tcount // (2 * NY)
    half = NY * block

    local = [pltpu.make_async_copy(qkv_hbm.at[i], wq.at[pl.ds(pl.multiple_of(ctx * share, share), share), pl.ds(i * width, width)], local_sem.at[i]) for i in range(3)]
    local.append(pltpu.make_async_copy(out_hbm, wo.at[ctx], local_sem.at[3]))
    local.append(pltpu.make_async_copy(tokens_hbm, tok, local_sem.at[4]))
    for copy in local:
        copy.start()

    after = {"ctx": lax.rem(ctx + 1, count)}
    partner = {"tp": tp + step}
    y_up = {"tp": lax.rem(y + step + NY, NY) * 2 + core}
    y_down = {"tp": lax.rem(y - step + NY, NY) * 2 + core}
    barrier = pltpu.get_barrier_semaphore()
    neighbours = [
        {"ctx": lax.rem(z + 1, NZ) * NX + x},
        {"ctx": lax.rem(z + NZ - 1, NZ) * NX + x},
        {"ctx": z * NX + lax.rem(x + 1, NX)},
        {"ctx": z * NX + lax.rem(x + NX - 1, NX)},
        after,
        {"ctx": lax.rem(ctx + count - 1, count)},
        partner,
        y_up,
        y_down,
    ]
    for device in neighbours:
        pl.semaphore_signal(barrier, inc=1, device_id=device, device_id_type=MESH)
    pl.semaphore_wait(barrier, len(neighbours))

    cut = 7 * 128
    ocut = 304

    def wq_slot(part, source):
        rows = pl.ds(pl.multiple_of(source * share, share), share)
        return wq.at[rows, pl.ds(0, cut)] if part == 0 else wq.at[rows, pl.ds(cut, 3 * width - cut)]

    def wo_slot(part, source):
        return wo.at[source, pl.ds(0, ocut), :] if part == 0 else wo.at[source, pl.ds(ocut, width - ocut), :]

    place = (z, x, step)
    wg = Gather(place, wq_slot, wq_ss, wq_rs)
    og = Gather(place, wo_slot, wo_ss, wo_rs)

    for copy in local[:3]:
        copy.wait()
    wg.begin()
    for copy in local[3:]:
        copy.wait()

    taps = long_ref.shape[1]
    lane = lax.broadcasted_iota(jnp.int32, (1, taps), 1).astype(jnp.float32)
    row_id = lax.broadcasted_iota(jnp.int32, (taps, taps), 0)
    col_id = lax.broadcasted_iota(jnp.int32, (taps, taps), 1)

    def build(group, carry):
        filt = long_ref[pl.ds(group, 1), :] * jnp.exp(-decay_ref[pl.ds(group, 1), :] * lane)
        ring = pltpu.roll(jnp.broadcast_to(filt, (taps, taps)), 0, 1, stride=1, stride_axis=0).T
        rows = pl.ds(pl.multiple_of(group * taps, taps), taps)
        band[rows, 0:taps] = jnp.where(col_id > row_id, ring, 0.0).astype(jnp.bfloat16)
        band[rows, taps : 2 * taps] = jnp.where(col_id <= row_id, ring, 0.0).astype(jnp.bfloat16)
        return carry

    lax.fori_loop(0, long_ref.shape[0], build, 0)

    lead = 8
    span = NX * share
    tile = 256

    def project(dz, first, last, part_of):
        source = lax.rem(z - step * dz + NZ, NZ)
        rows = pl.ds(pl.multiple_of(source * span, span), span)
        loops = 3 * width // tile // 2

        def one(n, carry):
            cols = pl.ds(pl.multiple_of((part_of * loops + n) * tile, tile), tile)
            part = jnp.dot(tok[:, rows], wq[rows, cols], preferred_element_type=jnp.float32)
            if not first:
                part = part + acc[lead:, cols]
            if last:
                part = part.astype(jnp.bfloat16).astype(jnp.float32)
            acc[lead:, cols] = part
            return carry

        lax.fori_loop(0, loops, one, 0)

    def remote(src, dst, ss, rs, device):
        return pltpu.make_async_remote_copy(src_ref=src, dst_ref=dst, send_sem=ss, recv_sem=rs, device_id=device, device_id_type=MESH)

    flight = {}

    def send_tail():
        tail_send[...] = acc[lead + tcount - 16 :, :].astype(jnp.bfloat16)
        flight["tail"] = remote(tail_send, tail_recv, halo_ss.at[0], halo_rs.at[0], after)
        flight["tail"].start()

    reach = short_ref.shape[1]
    lanes = 128

    def feature(s, r, c):
        cols = pl.ds(pl.multiple_of(s * width + c * lanes, lanes), lanes)
        own_cols = pl.ds(pl.multiple_of(c * lanes, lanes), lanes)
        window = acc[pl.ds(pl.multiple_of(r * taps, taps), taps + lead), cols]
        total = window[lead:] * short_ref[s, 0:1, own_cols]
        for j in range(1, reach):
            total = total + pltpu.roll(window, j, 0)[lead:] * short_ref[s, j : j + 1, own_cols]
        return total

    def features(r, c):
        rows = pl.ds(pl.multiple_of(r * taps, taps), taps)
        cols = pl.ds(pl.multiple_of(c * lanes, lanes), lanes)
        gat[pl.ds(pl.multiple_of(r * taps + taps, taps), taps), cols] = (feature(1, r, c) * feature(2, r, c)).astype(jnp.bfloat16)
        quer[rows, cols] = feature(0, r, c)

    tiles = width // lanes
    blocks = tcount // taps

    def feature_rows(r):
        lax.fori_loop(0, tiles, lambda c, k: (features(r, c), k)[1], 0)

    def send_halo():
        flight["halo"] = remote(gat.at[pl.ds(tcount, taps), :], halo, halo_ss.at[1], halo_rs.at[1], after)
        flight["halo"].start()

    def take_tail():
        flight["tail"].wait_recv()
        acc[0:lead, :] = jnp.where(ctx > 0, tail_recv[...].astype(jnp.float32)[16 - lead :, :], 0.0)

    def take_halo():
        flight["halo"].wait_recv()
        gat[0:taps, :] = jnp.where(ctx > 0, halo[...].astype(jnp.float32), 0.0).astype(jnp.bfloat16)

    group_of = lax.broadcasted_iota(jnp.int32, (taps, 2 * lanes), 1) % lanes // 16
    per_tile = lanes // 16

    def convolve(i, carry):
        p, c = lax.div(i, tiles), lax.rem(i, tiles)
        cols = pl.ds(pl.multiple_of(c * lanes, lanes), lanes)
        base = p * 2 * taps

        def at(offset, size):
            return pl.ds(pl.multiple_of(base + offset, taps), size)

        right = jnp.concatenate([gat[at(0, 2 * taps), cols], gat[at(taps, 2 * taps), cols]], axis=1)
        left = band[pl.ds(pl.multiple_of(c * per_tile * taps, taps), per_tile * taps), :]
        every = jnp.dot(left, right, preferred_element_type=jnp.float32)
        total = every[0:taps]
        for g in range(1, per_tile):
            total = jnp.where(group_of >= g, every[g * taps : (g + 1) * taps], total)
        gain = gain_ref[0:1, cols]
        for h in range(2):
            gated = gat[at((h + 1) * taps, taps), cols].astype(jnp.float32)
            rows = at(h * taps, taps)
            mix[rows, cols] = (quer[rows, cols] * (total[:, h * lanes : (h + 1) * lanes] + gain * gated)).astype(jnp.bfloat16)
        return carry

    def order_rows():
        for side in range(2):
            ahead = -step if side == 0 else step
            to_core = 1 - core if side == 0 else core
            for j in range(NY):
                to = lax.rem(y + ahead * j + NY, NY) * 2 + to_core
                mixp[side * half + j * block : side * half + (j + 1) * block, :] = mix[pl.ds(pl.multiple_of(to * block, 16), block), :]

    def stage0(k):
        offset, needs = CHUNKS[k]
        zsrc = lax.rem(z + offset, NZ)
        for i in range(NX // 2):
            right = jnp.concatenate([wo[zsrc * NX + 2 * i], wo[zsrc * NX + 2 * i + 1]], axis=1)
            cols = slice(2 * i * share, 2 * (i + 1) * share)
            cs_send[k, :, cols] = jnp.dot(mixp[0:half, :], right, preferred_element_type=jnp.float32).astype(jnp.bfloat16)
        copy = remote(cs_send.at[k], cs_recv.at[k], cs_ss.at[k], cs_rs.at[k], partner)
        copy.start()
        for i in range(NX // 2):
            right = jnp.concatenate([wo[zsrc * NX + 2 * i], wo[zsrc * NX + 2 * i + 1]], axis=1)
            cols = slice(2 * i * share, 2 * (i + 1) * share)
            own[k % 4, :, cols] = jnp.dot(mixp[half:, :], right, preferred_element_type=jnp.float32)
        return copy

    def rows_of(j):
        return slice(j * block, (j + 1) * block)

    def stage1(k):
        cs[k].wait_recv()
        slot = k % 4
        fs[k] = (own[slot, rows_of(2)] + cs_recv[k, rows_of(2)].astype(jnp.float32)).astype(jnp.bfloat16)
        first = remote(fs.at[k], fr.at[k], y_ss.at[0, k], y_rs.at[0, k], y_up)
        first.start()
        ms[k] = (own[slot, rows_of(3)] + cs_recv[k, rows_of(3)].astype(jnp.float32)).astype(jnp.bfloat16)
        minor = remote(ms.at[k], mr.at[k], y_ss.at[1, k], y_rs.at[1, k], y_down)
        minor.start()
        own[slot, 0 : 2 * block] = own[slot, 0 : 2 * block] + cs_recv[k, 0 : 2 * block].astype(jnp.float32)
        return first, minor

    def stage2(k):
        ys[k][0].wait_recv()
        js[k] = (own[k % 4, rows_of(1)] + fr[k].astype(jnp.float32)).astype(jnp.bfloat16)
        joined = remote(js.at[k], jr.at[k], y_ss.at[2, k], y_rs.at[2, k], y_up)
        joined.start()
        return joined

    def stage3(k):
        ys[k][1].wait_recv()
        jn[k].wait_recv()
        zsrc = lax.rem(z + CHUNKS[k][0], NZ)
        total = own[k % 4, rows_of(0)] + mr[k].astype(jnp.float32) + jr[k].astype(jnp.float32)
        result_ref[:, pl.ds(pl.multiple_of(zsrc * span, span), span)] = total.astype(jnp.bfloat16)

    cs, ys, jn = {}, {}, {}

    def stages(k):
        if k < NZ:
            cs[k] = stage0(k)
        if 1 <= k < NZ + 1:
            ys[k - 1] = stage1(k - 1)
        if 2 <= k < NZ + 2:
            jn[k - 2] = stage2(k - 2)
        if k >= 3:
            stage3(k - 3)

    def mixing():
        pairs = blocks // 2
        yield send_tail
        yield lambda: (feature_rows(blocks - 1), send_halo())
        for r in range(blocks - 2, 0, -1):
            yield lambda r=r: feature_rows(r)
        yield lambda: (take_tail(), feature_rows(0))
        for p in range(pairs - 1, -1, -1):
            if p == 0:
                yield take_halo
            yield lambda p=p: lax.fori_loop(p * tiles, p * tiles + tiles // 2, convolve, 0)
            yield lambda p=p: lax.fori_loop(p * tiles + tiles // 2, (p + 1) * tiles, convolve, 0)
        yield order_rows

    queue, seen, projected, chunk = [], {(p, 0, 0) for p in range(4)}, 0, 0
    ready = set()
    for code in ORDER:
        part, dz, dx = code // 32, code % 32 // 4, code % 4
        if code == 64:
            og.begin()
            continue
        (wg if part < 2 else og).arrive(part % 2, dz, dx)
        seen.add((part, dz, dx))
        if all((p, dz, i) in seen for p in (part // 2 * 2, part // 2 * 2 + 1) for i in range(NX)):
            if part < 2:
                projected += 1
                for i in range(2):
                    queue.append(lambda dz=dz, n=projected, i=i: project(dz, n == 1, n == NZ, i))
                if projected == NZ:
                    queue.extend(mixing())
            else:
                ready.add(dz)
        if projected == NZ:
            while chunk < NZ and ready >= set(CHUNKS[chunk][1]):
                queue.append(lambda k=chunk: stages(k))
                chunk += 1
        for _ in range(1 if projected < NZ else 2):
            if queue:
                queue.pop(0)()
    for piece in queue:
        piece()
    for k in range(NZ, NZ + 3):
        stages(k)

    wg.finish()
    og.finish()
    flight["tail"].wait_send()
    flight["halo"].wait_send()
    for k in range(NZ):
        cs[k].wait_send()
        ys[k][0].wait_send()
        ys[k][1].wait_send()
        jn[k].wait_send()


def per_device(tokens, qkv_weight, short_filter, long_filter, decay_rate, skip_gain, out_weight):
    tcount, depth = tokens.shape
    _, share, width = qkv_weight.shape
    taps = long_filter.shape[1]
    groups = long_filter.shape[0]
    span = NX * share
    block = tcount // (2 * NY)
    half = NY * block
    bf, f32 = jnp.bfloat16, jnp.float32
    dma = pltpu.SemaphoreType.DMA
    any_spec = pl.BlockSpec(memory_space=pl.ANY)
    vmem = pl.BlockSpec(memory_space=pltpu.VMEM)
    small = (NZ, block, span)
    return pl.pallas_call(
        kernel,
        out_shape=jax.ShapeDtypeStruct((block, depth), bf),
        in_specs=[any_spec, any_spec, vmem, vmem, vmem, vmem, any_spec],
        out_specs=vmem,
        scratch_shapes=[
            pltpu.VMEM((tcount, depth), bf),
            pltpu.VMEM((depth, 3 * width), bf),
            pltpu.VMEM((NZ * NX, width, share), bf),
            pltpu.VMEM((8 + tcount, 3 * width), f32),
            pltpu.VMEM((tcount, width), f32),
            pltpu.VMEM((taps + tcount, width), bf),
            pltpu.VMEM((groups * taps, 2 * taps), bf),
            pltpu.VMEM((tcount, width), bf),
            pltpu.VMEM((tcount, width), bf),
            pltpu.VMEM((4, half, span), f32),
            pltpu.VMEM((NZ, half, span), bf),
            pltpu.VMEM((NZ, half, span), bf),
            *[pltpu.VMEM(small, bf) for _ in range(6)],
            pltpu.VMEM((16, 3 * width), bf),
            pltpu.VMEM((16, 3 * width), bf),
            pltpu.VMEM((taps, width), bf),
            dma((5,)),
            dma((2, NZ, NX)),
            dma((2, NZ, NX)),
            dma((2, NZ, NX)),
            dma((2, NZ, NX)),
            dma((NZ,)),
            dma((NZ,)),
            dma((3, NZ)),
            dma((3, NZ)),
            dma((2,)),
            dma((2,)),
        ],
        compiler_params=pltpu.CompilerParams(
            collective_id=0, has_side_effects=True, vmem_limit_bytes=67043328
        ),
    )(
        tokens,
        qkv_weight,
        short_filter,
        long_filter,
        decay_rate[:, None],
        skip_gain[None, :],
        out_weight,
    )


def solution(mesh):
    in_specs = (
        P("ctx", None),
        P(None, "ctx", "tp"),
        P(None, None, "tp"),
        P("tp", None),
        P("tp"),
        P("tp"),
        P("tp", "ctx"),
    )
    out_specs = P(("ctx", "tp"), None)
    return jax.shard_map(
        per_device, mesh=mesh, in_specs=in_specs, out_specs=out_specs, check_vma=False
    )
```

```python
import jax
import jax.numpy as jnp
from jax import lax
from jax.experimental import pallas as pl
from jax.experimental.pallas import tpu as pltpu
from jax.sharding import PartitionSpec as P

MESH = pl.DeviceIdType.MESH
NZ, NX, NY = 8, 4, 4
ORDER = (
    4, 28, 33, 1, 36, 60, 200, 5, 8, 24, 29, 37, 61, 201, 9, 40, 56, 12, 20, 25, 41, 57, 64,
    202, 13, 44, 52, 97, 300, 300, 99, 300, 300, 300, 16, 53, 21, 300, 98, 92, 300, 300, 45,
    300, 68, 300, 300, 300, 300, 88, 48, 300, 300, 300, 17, 49, 301, 300, 72, 300, 300, 84, 300,
    300, 300, 65, 67, 300, 100, 124, 93, 95, 300, 69, 71, 300, 101, 125, 89, 91, 300, 73, 75,
    300, 103, 127, 85, 87, 66, 300, 102, 126, 94, 300, 70, 76, 120, 90, 300, 74, 104, 121, 86,
    300, 105, 300, 123, 107, 300, 77, 79, 122, 300, 106, 300, 116, 80, 117, 108, 78, 119, 109,
    118, 111, 81, 83, 300, 110, 300, 112, 300, 113, 115, 300, 82, 114, 300, 300, 300, 300, 300,
)
CHUNKS = ((0, (0,)), (1, (1, 7)), (7, (1, 7)), (2, (2, 6)), (6, (2, 6)), (3, (3, 5)), (5, (3, 5)), (4, (4,)))


class Gather:
    def __init__(self, place, slot, send_sem, recv_sem):
        self.z, self.x, self.step = place
        self.slot, self.send_sem, self.recv_sem = slot, send_sem, recv_sem
        self.sent, self.held = [], None

    def source(self, dz, dx):
        z = lax.rem(self.z - self.step * dz + NZ, NZ)
        x = lax.rem(self.x - self.step * dx + NX, NX)
        return z * NX + x

    def chip(self, axis, way):
        z, x = self.z, self.x
        if axis == "z":
            z = lax.rem(z + way * self.step + NZ, NZ)
        else:
            x = lax.rem(x + way * self.step + NX, NX)
        return z * NX + x

    def reach(self, dz, dx, axis, way):
        return ((dz + way) % NZ, dx) if axis == "z" else (dz, (dx + way) % NX)

    def transfer(self, part, dz, dx, index, device):
        ref = self.slot(part, self.source(dz, dx))
        return pltpu.make_async_remote_copy(
            src_ref=ref,
            dst_ref=ref,
            send_sem=self.send_sem.at[part, *index],
            recv_sem=self.recv_sem.at[part, *index],
            device_id={"ctx": device},
            device_id_type=MESH,
        )

    def send(self, part, dz, dx, axis, way):
        index = self.reach(dz, dx, axis, way)
        copy = self.transfer(part, dz, dx, index, self.chip(axis, way))
        copy.start()
        self.sent.append(copy)

    def wait(self, part, dz, dx):
        if (dz, dx) != (0, 0):
            self.transfer(part, dz, dx, (dz, dx), self.chip("z", 1)).wait_recv()

    def along_z(self, part, dz, dx):
        ways = [w for w, go in ((1, dz < NZ // 2), (-1, dz == 0 or dz > NZ // 2 + 1)) if go]
        return [(part, dz, dx, "z", w) for w in ways]

    def along_x(self, part, dz, dx):
        ways = [w for w, go in ((1, dx < NX // 2), (-1, dx == 0 or dx > NX // 2 + 1)) if go]
        return [(part, dz, dx, "x", w) for w in ways]

    def targets(self, part, dz, dx):
        if part == 0:
            return self.along_z(part, dz, dx) if dx == 0 else [], self.along_x(part, dz, dx)
        return self.along_x(part, dz, dx) if dz == 0 else [], self.along_z(part, dz, dx)

    def begin(self):
        both = [self.targets(part, 0, 0) for part in range(2)]
        for target in [t for pair in both for t in pair[0]]:
            self.send(*target)
        self.later([t for pair in both for t in pair[1]])

    def later(self, targets):
        if self.held is not None:
            self.held.extend(targets)
            return
        for target in targets:
            self.send(*target)

    def release(self):
        held, self.held = self.held, None
        self.later(held)

    def arrive(self, part, dz, dx):
        self.wait(part, dz, dx)
        first, second = self.targets(part, dz, dx)
        for target in first:
            self.send(*target)
        self.later(second)

    def finish(self):
        for copy in self.sent:
            copy.wait_send()


class PairGather(Gather):
    def __init__(self, place, logical, slot, send_sem, recv_sem, partner, psend_sem, precv_sem):
        super().__init__(place, slot, send_sem, recv_sem)
        self.kind = logical
        self.partner, self.psend_sem, self.precv_sem = partner, psend_sem, precv_sem

    def near(self, x):
        return x + 1 - 2 * lax.rem(x, 2)

    def source(self, dz, dx, step=None, kind=None):
        step = self.step if step is None else step
        kind = self.kind if kind is None else kind
        x = self.x if dx == 0 else self.near(self.x)
        return lax.rem(self.z - step * dz + NZ, NZ) * NX + x + kind * (NX - 1 - 2 * x)

    def chip(self, axis, way):
        if axis == "z":
            return super().chip(axis, way)
        return self.z * NX + self.near(self.x)

    def reach(self, dz, dx, axis, way):
        return super().reach(dz, dx, axis, way) if axis == "z" else (dz, 1)

    def along_x(self, part, dz, dx):
        return [(part, dz, dx, "x", 1)] if dx == 0 else []

    def across(self, part, dz, dx, source):
        ref = self.slot(part, source)
        return pltpu.make_async_remote_copy(
            src_ref=ref,
            dst_ref=ref,
            send_sem=self.psend_sem.at[part, dz, dx],
            recv_sem=self.precv_sem.at[part, dz, dx],
            device_id=self.partner,
            device_id_type=MESH,
        )

    def share(self, part, dz, dx):
        copy = self.across(part, dz, dx, self.source(dz, dx))
        copy.start()
        self.sent.append(copy)

    def begin(self):
        super().begin()
        for part in range(2):
            self.share(part, 0, 0)

    def arrive(self, part, dz, dx):
        super().arrive(part, dz, dx)
        self.share(part, dz, dx)

    def complete(self, dz):
        other = (NZ - dz) % NZ
        for part in range(2):
            for dx in range(2):
                source = self.source(other, dx, -self.step, 1 - self.kind)
                self.across(part, other, dx, source).wait_recv()


def kernel(
    tokens_hbm, qkv_hbm, short_in, long_in, decay_in, gain_in, out_hbm,
    result_ref, short_ref, long_ref, decay_ref, gain_ref,
    tok, wq, wo, acc, quer, gat, band, mix, mixr, mixp, own,
    cs_send, cs_recv, fs, fr, ms, mr, js, jr, tail_send, tail_recv, halo,
    local_sem, wq_ss, wq_rs, wo_ss, wo_rs, cs_ss, cs_rs, y_ss, y_rs, halo_ss, halo_rs,
    wp_ss, wp_rs, swap_ss, swap_rs, tok_ss, tok_rs, par_ss, par_rs, mix_ss, mix_rs,
):
    ctx, tp = lax.axis_index("ctx"), lax.axis_index("tp")
    z, x = lax.div(ctx, NX), lax.rem(ctx, NX)
    y, core = lax.div(tp, 2), lax.rem(tp, 2)
    step = 1 - 2 * core
    tcount, depth = tok.shape
    share = qkv_hbm.shape[1]
    width = qkv_hbm.shape[2]
    count = NZ * NX
    block = tcount // (2 * NY)
    half = NY * block

    side_of = lax.div(x, NX // 2)
    kind = lax.rem(core + side_of, 2)
    far = NX - 1 - x
    seat = x + kind * (NX - 1 - 2 * x)
    where = z * NX + seat

    def holder(row, col):
        other = lax.rem(lax.div(col, NX // 2) + side_of, 2)
        return {
            "ctx": row * NX + col + other * (NX - 1 - 2 * col),
            "tp": y * 2 + lax.rem(side_of + other, 2),
        }

    def remote(src, dst, ss, rs, device):
        return pltpu.make_async_remote_copy(src_ref=src, dst_ref=dst, send_sem=ss, recv_sem=rs, device_id=device, device_id_type=MESH)

    mate = {"ctx": z * NX + far, "tp": y * 2 + 1 - core}
    partner = {"tp": tp + step}
    params = ((short_in, short_ref), (long_in, long_ref), (decay_in, decay_ref), (gain_in, gain_ref))

    def shard_slot(source, i):
        return wq.at[pl.ds(pl.multiple_of(source * share, share), share), pl.ds(i * width, width)]

    def local_shard(i):
        return pltpu.make_async_copy(qkv_hbm.at[i], shard_slot(ctx, i), local_sem.at[i])

    def local_param(i):
        return pltpu.make_async_copy(*params[i], local_sem.at[5 + i])

    local_tok = pltpu.make_async_copy(tokens_hbm, tok, local_sem.at[4])
    local_out = pltpu.make_async_copy(out_hbm, wo.at[ctx], local_sem.at[3])

    @pl.when(kind == 0)
    def _():
        for i in range(3):
            local_shard(i).start()
        for i in range(4):
            local_param(i).start()
        local_tok.start()

    local_out.start()

    after = holder(lax.rem(z + lax.div(seat + 1, NX), NZ), lax.rem(seat + 1, NX))
    before = holder(lax.rem(z + NZ - 1 + lax.div(seat + NX - 1, NX), NZ), lax.rem(seat + NX - 1, NX))
    y_up = {"tp": lax.rem(y + step + NY, NY) * 2 + core}
    y_down = {"tp": lax.rem(y - step + NY, NY) * 2 + core}
    barrier = pltpu.get_barrier_semaphore()
    neighbours = [
        {"ctx": lax.rem(z + 1, NZ) * NX + x},
        {"ctx": lax.rem(z + NZ - 1, NZ) * NX + x},
        {"ctx": z * NX + lax.rem(x + 1, NX)},
        {"ctx": z * NX + lax.rem(x + NX - 1, NX)},
        after,
        before,
        mate,
        partner,
        y_up,
        y_down,
    ]
    for device in neighbours:
        pl.semaphore_signal(barrier, inc=1, device_id=device, device_id_type=MESH)
    pl.semaphore_wait(barrier, len(neighbours))

    cut = 6 * 128
    ocut = 208

    def wq_slot(part, source):
        rows = pl.ds(pl.multiple_of(source * share, share), share)
        return wq.at[rows, pl.ds(0, cut)] if part == 0 else wq.at[rows, pl.ds(cut, 3 * width - cut)]

    def wo_slot(part, source):
        return wo.at[source, pl.ds(0, ocut), :] if part == 0 else wo.at[source, pl.ds(ocut, width - ocut), :]

    place = (z, x, step)
    wg = PairGather(place, kind, wq_slot, wq_ss, wq_rs, partner, wp_ss, wp_rs)
    og = Gather(place, wo_slot, wo_ss, wo_rs)
    og.held = []

    def swap_shard(i, source):
        return remote(qkv_hbm.at[i], shard_slot(source, i), swap_ss.at[i], swap_rs.at[i], mate)

    def share_param(i):
        return remote(*params[i], par_ss.at[i], par_rs.at[i], partner)

    quarter = tcount // NY
    eighth = quarter // 2
    opposite = lax.rem(y + 2, NY)

    def token_rows(q, h, n):
        return pl.ds(pl.multiple_of(q * quarter + h * eighth, 16), n)

    def token_cross(i):
        rows = token_rows(y, i, eighth) if i < 2 else token_rows(opposite, 0, quarter)
        return remote(tokens_hbm.at[rows, :], tok.at[rows, :], tok_ss.at[i], tok_rs.at[i], mate)

    def token_pass(h, way, q):
        rows = token_rows(q, h, eighth)
        i = 3 + 2 * h + (0 if way > 0 else 1)
        to = {"tp": lax.rem(y + way + NY, NY) * 2 + core}
        return remote(tok.at[rows, :], tok.at[rows, :], tok_ss.at[i], tok_rs.at[i], to)

    def token_step(i):
        @pl.when(kind == 1)
        def _():
            if i < 2:
                token_cross(i).wait_recv()
                token_pass(i, 1, y).start()
                token_pass(i, -1, y).start()
            else:
                token_cross(2).wait_recv()
                for h in range(2):
                    for way in (1, -1):
                        token_pass(h, way, lax.rem(y - way + NY, NY)).wait_recv()

        if i == 2:
            @pl.when(kind == 0)
            def _():
                local_tok.wait()

    @pl.when(kind == 0)
    def _():
        for i in range(4):
            share_param(i).start()
        for i in range(3):
            local_shard(i).wait()

    @pl.when(kind == 1)
    def _():
        for i in range(3):
            swap_shard(i, ctx).start()
        for i in range(3):
            token_cross(i).start()
        for i in range(3):
            swap_shard(i, where).wait_recv()

    wg.begin()
    local_out.wait()

    @pl.when(kind == 0)
    def _():
        for i in range(4):
            local_param(i).wait()

    @pl.when(kind == 1)
    def _():
        for i in range(4):
            share_param(i).wait_recv()

    taps = long_ref.shape[1]
    lane = lax.broadcasted_iota(jnp.int32, (1, taps), 1).astype(jnp.float32)
    row_id = lax.broadcasted_iota(jnp.int32, (taps, taps), 0)
    col_id = lax.broadcasted_iota(jnp.int32, (taps, taps), 1)

    def build(group, carry):
        filt = long_ref[pl.ds(group, 1), :] * jnp.exp(-decay_ref[pl.ds(group, 1), :] * lane)
        ring = pltpu.roll(jnp.broadcast_to(filt, (taps, taps)), 0, 1, stride=1, stride_axis=0).T
        rows = pl.ds(pl.multiple_of(group * taps, taps), taps)
        band[rows, 0:taps] = jnp.where(col_id > row_id, ring, 0.0).astype(jnp.bfloat16)
        band[rows, taps : 2 * taps] = jnp.where(col_id <= row_id, ring, 0.0).astype(jnp.bfloat16)
        return carry

    lax.fori_loop(0, long_ref.shape[0], build, 0)

    lead = 8
    span = NX * share
    tile = 256

    def project(dz, first, last, part_of):
        source = lax.rem(z - step * dz + NZ, NZ)
        rows = pl.ds(pl.multiple_of(source * span, span), span)
        loops = 3 * width // tile // 3
        if part_of == 0:
            wg.complete(dz)

        def one(n, carry):
            cols = pl.ds(pl.multiple_of((part_of * loops + n) * tile, tile), tile)
            part = jnp.dot(tok[:, rows], wq[rows, cols], preferred_element_type=jnp.float32)
            if not first:
                part = part + acc[lead:, cols]
            if last:
                part = part.astype(jnp.bfloat16).astype(jnp.float32)
            acc[lead:, cols] = part
            return carry

        lax.fori_loop(0, loops, one, 0)

    flight = {}

    def send_tail():
        tail_send[...] = acc[lead + tcount - 16 :, :].astype(jnp.bfloat16)
        flight["tail"] = remote(tail_send, tail_recv, halo_ss.at[0], halo_rs.at[0], after)
        flight["tail"].start()

    reach = short_ref.shape[1]
    lanes = 128

    def feature(s, r, c):
        cols = pl.ds(pl.multiple_of(s * width + c * lanes, lanes), lanes)
        own_cols = pl.ds(pl.multiple_of(c * lanes, lanes), lanes)
        window = acc[pl.ds(pl.multiple_of(r * taps, taps), taps + lead), cols]
        total = window[lead:] * short_ref[s, 0:1, own_cols]
        for j in range(1, reach):
            total = total + pltpu.roll(window, j, 0)[lead:] * short_ref[s, j : j + 1, own_cols]
        return total

    def features(r, c):
        rows = pl.ds(pl.multiple_of(r * taps, taps), taps)
        cols = pl.ds(pl.multiple_of(c * lanes, lanes), lanes)
        gat[pl.ds(pl.multiple_of(r * taps + taps, taps), taps), cols] = (feature(1, r, c) * feature(2, r, c)).astype(jnp.bfloat16)
        quer[rows, cols] = feature(0, r, c)

    tiles = width // lanes
    blocks = tcount // taps

    def feature_rows(r):
        lax.fori_loop(0, tiles, lambda c, k: (features(r, c), k)[1], 0)

    def send_halo():
        flight["halo"] = remote(gat.at[pl.ds(tcount, taps), :], halo, halo_ss.at[1], halo_rs.at[1], after)
        flight["halo"].start()

    def take_tail():
        flight["tail"].wait_recv()
        acc[0:lead, :] = jnp.where(where > 0, tail_recv[...].astype(jnp.float32)[16 - lead :, :], 0.0)

    def take_halo():
        flight["halo"].wait_recv()
        gat[0:taps, :] = jnp.where(where > 0, halo[...].astype(jnp.float32), 0.0).astype(jnp.bfloat16)

    group_of = lax.broadcasted_iota(jnp.int32, (taps, 2 * lanes), 1) % lanes // 16
    per_tile = lanes // 16

    def convolve(i, carry):
        p, c = lax.div(i, tiles), lax.rem(i, tiles)
        cols = pl.ds(pl.multiple_of(c * lanes, lanes), lanes)
        base = p * 2 * taps

        def at(offset, size):
            return pl.ds(pl.multiple_of(base + offset, taps), size)

        right = jnp.concatenate([gat[at(0, 2 * taps), cols], gat[at(taps, 2 * taps), cols]], axis=1)
        left = band[pl.ds(pl.multiple_of(c * per_tile * taps, taps), per_tile * taps), :]
        every = jnp.dot(left, right, preferred_element_type=jnp.float32)
        total = every[0:taps]
        for g in range(1, per_tile):
            total = jnp.where(group_of >= g, every[g * taps : (g + 1) * taps], total)
        gain = gain_ref[0:1, cols]
        for h in range(2):
            gated = gat[at((h + 1) * taps, taps), cols].astype(jnp.float32)
            rows = at(h * taps, taps)
            mix[rows, cols] = (quer[rows, cols] * (total[:, h * lanes : (h + 1) * lanes] + gain * gated)).astype(jnp.bfloat16)
        return carry

    def mix_copy(p):
        rows = pl.ds(p * 2 * taps, 2 * taps)
        return remote(mix.at[rows, :], mixr.at[rows, :], mix_ss.at[p], mix_rs.at[p], mate)

    def send_mix(p):
        @pl.when(kind == 1)
        def _():
            mix_copy(p).start()

    def order_rows():
        def fill(rows_from):
            for side in range(2):
                ahead = -step if side == 0 else step
                to_core = 1 - core if side == 0 else core
                for j in range(NY):
                    to = lax.rem(y + ahead * j + NY, NY) * 2 + to_core
                    mixp[side * half + j * block : side * half + (j + 1) * block, :] = rows_from[pl.ds(pl.multiple_of(to * block, 16), block), :]

        @pl.when(kind == 0)
        def _():
            fill(mix)

        @pl.when(kind == 1)
        def _():
            for p in range(blocks // 2):
                mix_copy(p).wait_recv()
            fill(mixr)

    def stage0(k):
        offset, needs = CHUNKS[k]
        zsrc = lax.rem(z + offset, NZ)
        for i in range(NX // 2):
            right = jnp.concatenate([wo[zsrc * NX + 2 * i], wo[zsrc * NX + 2 * i + 1]], axis=1)
            cols = slice(2 * i * share, 2 * (i + 1) * share)
            cs_send[k, :, cols] = jnp.dot(mixp[0:half, :], right, preferred_element_type=jnp.float32).astype(jnp.bfloat16)
        copy = remote(cs_send.at[k], cs_recv.at[k], cs_ss.at[k], cs_rs.at[k], partner)
        copy.start()
        for i in range(NX // 2):
            right = jnp.concatenate([wo[zsrc * NX + 2 * i], wo[zsrc * NX + 2 * i + 1]], axis=1)
            cols = slice(2 * i * share, 2 * (i + 1) * share)
            own[k % 4, :, cols] = jnp.dot(mixp[half:, :], right, preferred_element_type=jnp.float32)
        return copy

    def rows_of(j):
        return slice(j * block, (j + 1) * block)

    def stage1(k):
        cs[k].wait_recv()
        slot = k % 4
        fs[k] = (own[slot, rows_of(2)] + cs_recv[k, rows_of(2)].astype(jnp.float32)).astype(jnp.bfloat16)
        first = remote(fs.at[k], fr.at[k], y_ss.at[0, k], y_rs.at[0, k], y_up)
        first.start()
        ms[k] = (own[slot, rows_of(3)] + cs_recv[k, rows_of(3)].astype(jnp.float32)).astype(jnp.bfloat16)
        minor = remote(ms.at[k], mr.at[k], y_ss.at[1, k], y_rs.at[1, k], y_down)
        minor.start()
        own[slot, 0 : 2 * block] = own[slot, 0 : 2 * block] + cs_recv[k, 0 : 2 * block].astype(jnp.float32)
        return first, minor

    def stage2(k):
        ys[k][0].wait_recv()
        js[k] = (own[k % 4, rows_of(1)] + fr[k].astype(jnp.float32)).astype(jnp.bfloat16)
        joined = remote(js.at[k], jr.at[k], y_ss.at[2, k], y_rs.at[2, k], y_up)
        joined.start()
        return joined

    def stage3(k):
        ys[k][1].wait_recv()
        jn[k].wait_recv()
        zsrc = lax.rem(z + CHUNKS[k][0], NZ)
        total = own[k % 4, rows_of(0)] + mr[k].astype(jnp.float32) + jr[k].astype(jnp.float32)
        result_ref[:, pl.ds(pl.multiple_of(zsrc * span, span), span)] = total.astype(jnp.bfloat16)

    cs, ys, jn = {}, {}, {}

    def stages(k):
        if k < NZ:
            cs[k] = stage0(k)
        if 1 <= k < NZ + 1:
            ys[k - 1] = stage1(k - 1)
        if 2 <= k < NZ + 2:
            jn[k - 2] = stage2(k - 2)
        if k >= 3:
            stage3(k - 3)

    def mixing():
        def conv(p):
            lax.fori_loop(p * tiles, (p + 1) * tiles, convolve, 0)
            send_mix(p)

        yield send_tail
        yield lambda: (feature_rows(blocks - 1), send_halo())
        for r in range(blocks - 2, 0, -1):
            yield lambda r=r: feature_rows(r)
            if r % 2 == 1:
                yield lambda p=r // 2 + 1: conv(p)
        yield lambda: (take_tail(), feature_rows(0))
        yield take_halo
        yield lambda: conv(0)
        yield order_rows

    queue, seen, projected, chunk = [], {(p, 0, 0) for p in range(4)}, 0, 0
    ready, tokens_in = set(), False
    waiting = [0, 1, 7, 2, 6, 3, 5, 4]
    for code in ORDER:
        if code == 64:
            og.begin()
            continue
        if code == 301:
            og.release()
            continue
        if code == 300:
            queue.pop(0)()
            continue
        if code >= 200:
            token_step(code - 200)
            tokens_in = code == 202
        else:
            part, dz, dx = code // 32, code % 32 // 4, code % 4
            (wg if part < 2 else og).arrive(part % 2, dz, dx)
            seen.add((part, dz, dx))
            if part >= 2 and all((p, dz, i) in seen for p in (2, 3) for i in range(NX)):
                ready.add(dz)
        while tokens_in and waiting:
            dz = waiting[0]
            twins = (dz, (NZ - dz) % NZ)
            if not all((p, d, i) in seen for p in (0, 1) for d in twins for i in range(2)):
                break
            waiting.pop(0)
            projected += 1
            for i in range(3):
                queue.append(lambda dz=dz, n=projected, i=i: project(dz, n == 1, n == NZ, i))
            if projected == NZ:
                queue.extend(mixing())
        if projected == NZ:
            while chunk < NZ and ready >= set(CHUNKS[chunk][1]):
                queue.append(lambda k=chunk: stages(k))
                chunk += 1
    for piece in queue:
        piece()
    for k in range(NZ, NZ + 3):
        stages(k)

    wg.finish()
    og.finish()
    flight["tail"].wait_send()
    flight["halo"].wait_send()
    for k in range(NZ):
        cs[k].wait_send()
        ys[k][0].wait_send()
        ys[k][1].wait_send()
        jn[k].wait_send()

    @pl.when(kind == 0)
    def _():
        for i in range(4):
            share_param(i).wait_send()

    @pl.when(kind == 1)
    def _():
        for i in range(3):
            swap_shard(i, ctx).wait_send()
            token_cross(i).wait_send()
            mix_copy(i).wait_send()
        for h in range(2):
            token_pass(h, 1, y).wait_send()
            token_pass(h, -1, y).wait_send()


def per_device(tokens, qkv_weight, short_filter, long_filter, decay_rate, skip_gain, out_weight):
    tcount, depth = tokens.shape
    _, share, width = qkv_weight.shape
    taps = long_filter.shape[1]
    groups = long_filter.shape[0]
    span = NX * share
    block = tcount // (2 * NY)
    half = NY * block
    bf, f32 = jnp.bfloat16, jnp.float32
    dma = pltpu.SemaphoreType.DMA
    any_spec = pl.BlockSpec(memory_space=pl.ANY)
    vmem = pl.BlockSpec(memory_space=pltpu.VMEM)
    small = (NZ, block, span)
    return pl.pallas_call(
        kernel,
        out_shape=jax.ShapeDtypeStruct((block, depth), bf),
        in_specs=[any_spec, any_spec, vmem, vmem, vmem, vmem, any_spec],
        out_specs=vmem,
        scratch_shapes=[
            pltpu.VMEM(short_filter.shape, f32),
            pltpu.VMEM(long_filter.shape, f32),
            pltpu.VMEM((groups, 1), f32),
            pltpu.VMEM((1, width), f32),
            pltpu.VMEM((tcount, depth), bf),
            pltpu.VMEM((depth, 3 * width), bf),
            pltpu.VMEM((NZ * NX, width, share), bf),
            pltpu.VMEM((8 + tcount, 3 * width), f32),
            pltpu.VMEM((tcount, width), f32),
            pltpu.VMEM((taps + tcount, width), bf),
            pltpu.VMEM((groups * taps, 2 * taps), bf),
            pltpu.VMEM((tcount, width), bf),
            pltpu.VMEM((tcount, width), bf),
            pltpu.VMEM((tcount, width), bf),
            pltpu.VMEM((4, half, span), f32),
            pltpu.VMEM((NZ, half, span), bf),
            pltpu.VMEM((NZ, half, span), bf),
            *[pltpu.VMEM(small, bf) for _ in range(6)],
            pltpu.VMEM((16, 3 * width), bf),
            pltpu.VMEM((16, 3 * width), bf),
            pltpu.VMEM((taps, width), bf),
            dma((9,)),
            dma((2, NZ, 2)),
            dma((2, NZ, 2)),
            dma((2, NZ, NX)),
            dma((2, NZ, NX)),
            dma((NZ,)),
            dma((NZ,)),
            dma((3, NZ)),
            dma((3, NZ)),
            dma((2,)),
            dma((2,)),
            dma((2, NZ, 2)),
            dma((2, NZ, 2)),
            dma((3,)),
            dma((3,)),
            dma((7,)),
            dma((7,)),
            dma((4,)),
            dma((4,)),
            dma((3,)),
            dma((3,)),
        ],
        compiler_params=pltpu.CompilerParams(
            collective_id=0, has_side_effects=True, vmem_limit_bytes=67043328
        ),
    )(
        tokens,
        qkv_weight,
        short_filter,
        long_filter,
        decay_rate[:, None],
        skip_gain[None, :],
        out_weight,
    )


def solution(mesh):
    in_specs = (
        P("ctx", None),
        P(None, "ctx", "tp"),
        P(None, None, "tp"),
        P("tp", None),
        P("tp"),
        P("tp"),
        P("tp", "ctx"),
    )
    out_specs = P(("ctx", "tp"), None)
    return jax.shard_map(
        per_device, mesh=mesh, in_specs=in_specs, out_specs=out_specs, check_vma=False
    )
```

```python
import jax
import jax.numpy as jnp
from jax import lax
from jax.experimental import pallas as pl
from jax.experimental.pallas import tpu as pltpu
from jax.sharding import PartitionSpec as P

MESH = pl.DeviceIdType.MESH
NZ, NX, NY = 8, 4, 4
ORDER = (
    4, 28, 33, 200, 1, 36, 60, 201, 5, 8, 24, 202, 29, 37, 61, 203, 9, 40, 56, 12, 20, 25, 41,
    57, 64, 204, 13, 44, 52, 300, 300, 300, 300, 97, 300, 99, 300, 16, 53, 21, 300, 300, 300,
    300, 45, 92, 300, 300, 300, 300, 68, 98, 48, 300, 300, 300, 17, 300, 300, 49, 301, 300, 88,
    300, 72, 300, 300, 300, 300, 300, 300, 300, 65, 67, 300, 100, 124, 93, 95, 69, 71, 300, 101,
    125, 89, 91, 300, 73, 75, 103, 127, 300, 300, 102, 126, 66, 300, 76, 84, 300, 94, 104, 120,
    70, 90, 105, 121, 74, 107, 123, 300, 77, 79, 106, 122, 85, 87, 80, 300, 108, 116, 300, 109,
    117, 300, 111, 119, 78, 83, 86, 300, 110, 118, 81, 112, 300, 113, 300, 115, 300, 114, 82,
    300,
)
CHUNKS = ((0, (0,)), (1, (1, 7)), (7, (1, 7)), (2, (2, 6)), (6, (2, 6)), (3, (3, 5)), (5, (3, 5)), (4, (4,)))


class Gather:
    def __init__(self, place, slot, send_sem, recv_sem):
        self.z, self.x, self.step = place
        self.slot, self.send_sem, self.recv_sem = slot, send_sem, recv_sem
        self.sent, self.held = [], None

    def source(self, dz, dx):
        z = lax.rem(self.z - self.step * dz + NZ, NZ)
        x = lax.rem(self.x - self.step * dx + NX, NX)
        return z * NX + x

    def chip(self, axis, way):
        z, x = self.z, self.x
        if axis == "z":
            z = lax.rem(z + way * self.step + NZ, NZ)
        else:
            x = lax.rem(x + way * self.step + NX, NX)
        return z * NX + x

    def reach(self, dz, dx, axis, way):
        return ((dz + way) % NZ, dx) if axis == "z" else (dz, (dx + way) % NX)

    def transfer(self, part, dz, dx, index, device):
        ref = self.slot(part, self.source(dz, dx))
        return pltpu.make_async_remote_copy(
            src_ref=ref,
            dst_ref=ref,
            send_sem=self.send_sem.at[part, *index],
            recv_sem=self.recv_sem.at[part, *index],
            device_id={"ctx": device},
            device_id_type=MESH,
        )

    def send(self, part, dz, dx, axis, way):
        index = self.reach(dz, dx, axis, way)
        copy = self.transfer(part, dz, dx, index, self.chip(axis, way))
        copy.start()
        self.sent.append(copy)

    def wait(self, part, dz, dx):
        if (dz, dx) != (0, 0):
            self.transfer(part, dz, dx, (dz, dx), self.chip("z", 1)).wait_recv()

    def along_z(self, part, dz, dx):
        ways = [w for w, go in ((1, dz < NZ // 2), (-1, dz == 0 or dz > NZ // 2 + 1)) if go]
        return [(part, dz, dx, "z", w) for w in ways]

    def along_x(self, part, dz, dx):
        ways = [w for w, go in ((1, dx < NX // 2), (-1, dx == 0 or dx > NX // 2 + 1)) if go]
        return [(part, dz, dx, "x", w) for w in ways]

    def targets(self, part, dz, dx):
        if part == 0:
            return self.along_z(part, dz, dx) if dx == 0 else [], self.along_x(part, dz, dx)
        return self.along_x(part, dz, dx) if dz == 0 else [], self.along_z(part, dz, dx)

    def begin(self):
        both = [self.targets(part, 0, 0) for part in range(2)]
        for target in [t for pair in both for t in pair[0]]:
            self.send(*target)
        self.later([t for pair in both for t in pair[1]])

    def later(self, targets):
        if self.held is not None:
            self.held.extend(targets)
            return
        for target in targets:
            self.send(*target)

    def release(self):
        held, self.held = self.held, None
        self.later(held)

    def arrive(self, part, dz, dx):
        self.wait(part, dz, dx)
        first, second = self.targets(part, dz, dx)
        for target in first:
            self.send(*target)
        self.later(second)

    def finish(self):
        for copy in self.sent:
            copy.wait_send()


class PairGather(Gather):
    def __init__(self, place, logical, slot, send_sem, recv_sem, partner, psend_sem, precv_sem):
        super().__init__(place, slot, send_sem, recv_sem)
        self.kind = logical
        self.partner, self.psend_sem, self.precv_sem = partner, psend_sem, precv_sem

    def near(self, x):
        return x + 1 - 2 * lax.rem(x, 2)

    def source(self, dz, dx, step=None, kind=None):
        step = self.step if step is None else step
        kind = self.kind if kind is None else kind
        x = self.x if dx == 0 else self.near(self.x)
        return lax.rem(self.z - step * dz + NZ, NZ) * NX + x + kind * (NX - 1 - 2 * x)

    def chip(self, axis, way):
        if axis == "z":
            return super().chip(axis, way)
        return self.z * NX + self.near(self.x)

    def reach(self, dz, dx, axis, way):
        return super().reach(dz, dx, axis, way) if axis == "z" else (dz, 1)

    def along_x(self, part, dz, dx):
        return [(part, dz, dx, "x", 1)] if dx == 0 else []

    def across(self, part, dz, dx, source):
        ref = self.slot(part, source)
        return pltpu.make_async_remote_copy(
            src_ref=ref,
            dst_ref=ref,
            send_sem=self.psend_sem.at[part, dz, dx],
            recv_sem=self.precv_sem.at[part, dz, dx],
            device_id=self.partner,
            device_id_type=MESH,
        )

    def share(self, part, dz, dx):
        copy = self.across(part, dz, dx, self.source(dz, dx))
        copy.start()
        self.sent.append(copy)

    def begin(self):
        super().begin()
        for part in range(2):
            self.share(part, 0, 0)

    def arrive(self, part, dz, dx):
        super().arrive(part, dz, dx)
        self.share(part, dz, dx)

    def complete(self, dz):
        other = (NZ - dz) % NZ
        for part in range(2):
            for dx in range(2):
                source = self.source(other, dx, -self.step, 1 - self.kind)
                self.across(part, other, dx, source).wait_recv()


def kernel(
    tokens_hbm, qkv_hbm, short_in, long_in, decay_in, gain_in, out_hbm,
    result_ref, short_ref, long_ref, decay_ref, gain_ref,
    tok, wq, wo, acc, quer, gat, band, mix, mixr, mixp, own,
    cs_send, cs_recv, fs, fr, ms, mr, js, jr, tail_send, tail_recv, halo,
    local_sem, wq_ss, wq_rs, wo_ss, wo_rs, cs_ss, cs_rs, y_ss, y_rs, halo_ss, halo_rs,
    wp_ss, wp_rs, swap_ss, swap_rs, tok_ss, tok_rs, par_ss, par_rs, mix_ss, mix_rs,
):
    ctx, tp = lax.axis_index("ctx"), lax.axis_index("tp")
    z, x = lax.div(ctx, NX), lax.rem(ctx, NX)
    y, core = lax.div(tp, 2), lax.rem(tp, 2)
    step = 1 - 2 * core
    tcount, depth = tok.shape
    share = qkv_hbm.shape[1]
    width = qkv_hbm.shape[2]
    count = NZ * NX
    block = tcount // (2 * NY)
    half = NY * block

    side_of = lax.div(x, NX // 2)
    kind = lax.rem(core + side_of, 2)
    far = NX - 1 - x
    seat = x + kind * (NX - 1 - 2 * x)
    where = z * NX + seat

    def holder(row, col):
        other = lax.rem(lax.div(col, NX // 2) + side_of, 2)
        return {
            "ctx": row * NX + col + other * (NX - 1 - 2 * col),
            "tp": y * 2 + lax.rem(side_of + other, 2),
        }

    def remote(src, dst, ss, rs, device):
        return pltpu.make_async_remote_copy(src_ref=src, dst_ref=dst, send_sem=ss, recv_sem=rs, device_id=device, device_id_type=MESH)

    mate = {"ctx": z * NX + far, "tp": y * 2 + 1 - core}
    partner = {"tp": tp + step}
    params = ((short_in, short_ref), (long_in, long_ref), (decay_in, decay_ref), (gain_in, gain_ref))

    def shard_slot(source, i):
        return wq.at[pl.ds(pl.multiple_of(source * share, share), share), pl.ds(i * width, width)]

    def local_shard(i):
        return pltpu.make_async_copy(qkv_hbm.at[i], shard_slot(ctx, i), local_sem.at[i])

    def local_param(i):
        return pltpu.make_async_copy(*params[i], local_sem.at[5 + i])

    local_tok = pltpu.make_async_copy(tokens_hbm, tok, local_sem.at[4])
    local_out = pltpu.make_async_copy(out_hbm, wo.at[ctx], local_sem.at[3])

    @pl.when(kind == 0)
    def _():
        for i in range(3):
            local_shard(i).start()
        for i in range(4):
            local_param(i).start()
        local_tok.start()

    local_out.start()

    after = holder(lax.rem(z + lax.div(seat + 1, NX), NZ), lax.rem(seat + 1, NX))
    before = holder(lax.rem(z + NZ - 1 + lax.div(seat + NX - 1, NX), NZ), lax.rem(seat + NX - 1, NX))
    y_up = {"tp": lax.rem(y + step + NY, NY) * 2 + core}
    y_down = {"tp": lax.rem(y - step + NY, NY) * 2 + core}
    barrier = pltpu.get_barrier_semaphore()
    neighbours = [
        {"ctx": lax.rem(z + 1, NZ) * NX + x},
        {"ctx": lax.rem(z + NZ - 1, NZ) * NX + x},
        {"ctx": z * NX + lax.rem(x + 1, NX)},
        {"ctx": z * NX + lax.rem(x + NX - 1, NX)},
        after,
        before,
        mate,
        partner,
        y_up,
        y_down,
    ]
    for device in neighbours:
        pl.semaphore_signal(barrier, inc=1, device_id=device, device_id_type=MESH)
    pl.semaphore_wait(barrier, len(neighbours))

    cut = 6 * 128
    ocut = 208

    def wq_slot(part, source):
        rows = pl.ds(pl.multiple_of(source * share, share), share)
        return wq.at[rows, pl.ds(0, cut)] if part == 0 else wq.at[rows, pl.ds(cut, 3 * width - cut)]

    def wo_slot(part, source):
        return wo.at[source, pl.ds(0, ocut), :] if part == 0 else wo.at[source, pl.ds(ocut, width - ocut), :]

    place = (z, x, step)
    wg = PairGather(place, kind, wq_slot, wq_ss, wq_rs, partner, wp_ss, wp_rs)
    og = Gather(place, wo_slot, wo_ss, wo_rs)
    og.held = []

    def swap_shard(i, source):
        return remote(qkv_hbm.at[i], shard_slot(source, i), swap_ss.at[i], swap_rs.at[i], mate)

    def share_param(i):
        return remote(*params[i], par_ss.at[i], par_rs.at[i], partner)

    quarter = tcount // NY
    part_rows = quarter // 4
    opposite = lax.rem(y + 2, NY)

    def token_rows(q, h, n):
        return pl.ds(pl.multiple_of(q * quarter + h * part_rows, 16), n)

    def token_cross(i):
        rows = token_rows(y, i, part_rows) if i < 4 else token_rows(opposite, 2, 2 * part_rows)
        return remote(tokens_hbm.at[rows, :], tok.at[rows, :], tok_ss.at[i], tok_rs.at[i], mate)

    def along_y(rows, i, way):
        to = {"tp": lax.rem(y + way + NY, NY) * 2 + core}
        return remote(tok.at[rows, :], tok.at[rows, :], tok_ss.at[i], tok_rs.at[i], to)

    def token_pass(h, way, q):
        return along_y(token_rows(q, h, part_rows), 5 + 2 * h + (way < 0), way)

    def token_relay(way, q):
        return along_y(token_rows(q, int(way > 0), part_rows), 13 + (way < 0), way)

    def from_side(way):
        return lax.rem(y - way + NY, NY)

    def token_step(i):
        @pl.when(kind == 1)
        def _():
            if i < 4:
                token_cross(i).wait_recv()
                token_pass(i, 1, y).start()
                token_pass(i, -1, y).start()
                if i >= 2:
                    way = -1 if i == 2 else 1
                    token_pass(i - 2, way, from_side(way)).wait_recv()
                    token_relay(way, from_side(way)).start()
            else:
                token_cross(4).wait_recv()
                for way in (1, -1):
                    for h in range(4):
                        if (h, way) not in ((0, -1), (1, 1)):
                            token_pass(h, way, from_side(way)).wait_recv()
                    token_relay(way, opposite).wait_recv()

        if i == 4:
            @pl.when(kind == 0)
            def _():
                local_tok.wait()

    @pl.when(kind == 0)
    def _():
        for i in range(4):
            share_param(i).start()
        for i in range(3):
            local_shard(i).wait()

    @pl.when(kind == 1)
    def _():
        for i in range(3):
            swap_shard(i, ctx).start()
        for i in range(5):
            token_cross(i).start()
        for i in range(3):
            swap_shard(i, where).wait_recv()

    wg.begin()
    local_out.wait()

    @pl.when(kind == 0)
    def _():
        for i in range(4):
            local_param(i).wait()

    @pl.when(kind == 1)
    def _():
        for i in range(4):
            share_param(i).wait_recv()

    taps = long_ref.shape[1]
    lane = lax.broadcasted_iota(jnp.int32, (1, taps), 1).astype(jnp.float32)
    group_id = lax.broadcasted_iota(jnp.int32, decay_ref.shape, 1)
    row_id = lax.broadcasted_iota(jnp.int32, (taps, taps), 0)
    col_id = lax.broadcasted_iota(jnp.int32, (taps, taps), 1)

    def build(group, carry):
        rate = jnp.sum(jnp.where(group_id == group, decay_ref[...], 0.0), axis=1, keepdims=True)
        filt = long_ref[pl.ds(group, 1), :] * jnp.exp(-rate * lane)
        ring = pltpu.roll(jnp.broadcast_to(filt, (taps, taps)), 0, 1, stride=1, stride_axis=0).T
        rows = pl.ds(pl.multiple_of(group * taps, taps), taps)
        band[rows, 0:taps] = jnp.where(col_id > row_id, ring, 0.0).astype(jnp.bfloat16)
        band[rows, taps : 2 * taps] = jnp.where(col_id <= row_id, ring, 0.0).astype(jnp.bfloat16)
        return carry

    lax.fori_loop(0, long_ref.shape[0], build, 0)

    lead = 8
    span = NX * share
    tile = 256

    def project(dz, first, last, part_of):
        source = lax.rem(z - step * dz + NZ, NZ)
        rows = pl.ds(pl.multiple_of(source * span, span), span)
        loops = 3 * width // tile // 3
        if part_of == 0:
            wg.complete(dz)

        def one(n, carry):
            cols = pl.ds(pl.multiple_of((part_of * loops + n) * tile, tile), tile)
            part = jnp.dot(tok[:, rows], wq[rows, cols], preferred_element_type=jnp.float32)
            if not first:
                part = part + acc[lead:, cols]
            if last:
                part = part.astype(jnp.bfloat16).astype(jnp.float32)
            acc[lead:, cols] = part
            return carry

        lax.fori_loop(0, loops, one, 0)

    flight = {}

    def send_tail():
        tail_send[...] = acc[lead + tcount - 16 :, :].astype(jnp.bfloat16)
        flight["tail"] = remote(tail_send, tail_recv, halo_ss.at[0], halo_rs.at[0], after)
        flight["tail"].start()

    reach = short_ref.shape[1]
    lanes = 128

    def feature(s, r, c):
        cols = pl.ds(pl.multiple_of(s * width + c * lanes, lanes), lanes)
        own_cols = pl.ds(pl.multiple_of(c * lanes, lanes), lanes)
        window = acc[pl.ds(pl.multiple_of(r * taps, taps), taps + lead), cols]
        total = window[lead:] * short_ref[s, 0:1, own_cols]
        for j in range(1, reach):
            total = total + pltpu.roll(window, j, 0)[lead:] * short_ref[s, j : j + 1, own_cols]
        return total

    def features(r, c):
        rows = pl.ds(pl.multiple_of(r * taps, taps), taps)
        cols = pl.ds(pl.multiple_of(c * lanes, lanes), lanes)
        gat[pl.ds(pl.multiple_of(r * taps + taps, taps), taps), cols] = (feature(1, r, c) * feature(2, r, c)).astype(jnp.bfloat16)
        quer[rows, cols] = feature(0, r, c)

    tiles = width // lanes
    blocks = tcount // taps

    def feature_rows(r):
        lax.fori_loop(0, tiles, lambda c, k: (features(r, c), k)[1], 0)

    def send_halo():
        flight["halo"] = remote(gat.at[pl.ds(tcount, taps), :], halo, halo_ss.at[1], halo_rs.at[1], after)
        flight["halo"].start()

    def take_tail():
        flight["tail"].wait_recv()
        acc[0:lead, :] = jnp.where(where > 0, tail_recv[...].astype(jnp.float32)[16 - lead :, :], 0.0)

    def take_halo():
        flight["halo"].wait_recv()
        gat[0:taps, :] = jnp.where(where > 0, halo[...].astype(jnp.float32), 0.0).astype(jnp.bfloat16)

    group_of = lax.broadcasted_iota(jnp.int32, (taps, 2 * lanes), 1) % lanes // 16
    per_tile = lanes // 16

    def convolve(i, carry):
        p, c = lax.div(i, tiles), lax.rem(i, tiles)
        cols = pl.ds(pl.multiple_of(c * lanes, lanes), lanes)
        base = p * 2 * taps

        def at(offset, size):
            return pl.ds(pl.multiple_of(base + offset, taps), size)

        right = jnp.concatenate([gat[at(0, 2 * taps), cols], gat[at(taps, 2 * taps), cols]], axis=1)
        left = band[pl.ds(pl.multiple_of(c * per_tile * taps, taps), per_tile * taps), :]
        every = jnp.dot(left, right, preferred_element_type=jnp.float32)
        total = every[0:taps]
        for g in range(1, per_tile):
            total = jnp.where(group_of >= g, every[g * taps : (g + 1) * taps], total)
        gain = gain_ref[0:1, cols]
        for h in range(2):
            gated = gat[at((h + 1) * taps, taps), cols].astype(jnp.float32)
            rows = at(h * taps, taps)
            mix[rows, cols] = (quer[rows, cols] * (total[:, h * lanes : (h + 1) * lanes] + gain * gated)).astype(jnp.bfloat16)
        return carry

    def mix_copy(p):
        rows = pl.ds(p * 2 * taps, 2 * taps)
        return remote(mix.at[rows, :], mixr.at[rows, :], mix_ss.at[p], mix_rs.at[p], mate)

    def send_mix(p):
        @pl.when(kind == 1)
        def _():
            mix_copy(p).start()

    def order_rows():
        def fill(rows_from):
            for side in range(2):
                ahead = -step if side == 0 else step
                to_core = 1 - core if side == 0 else core
                for j in range(NY):
                    to = lax.rem(y + ahead * j + NY, NY) * 2 + to_core
                    mixp[side * half + j * block : side * half + (j + 1) * block, :] = rows_from[pl.ds(pl.multiple_of(to * block, 16), block), :]

        @pl.when(kind == 0)
        def _():
            fill(mix)

        @pl.when(kind == 1)
        def _():
            for p in range(blocks // 2):
                mix_copy(p).wait_recv()
            fill(mixr)

    def stage0(k):
        offset, needs = CHUNKS[k]
        zsrc = lax.rem(z + offset, NZ)
        for i in range(NX // 2):
            right = jnp.concatenate([wo[zsrc * NX + 2 * i], wo[zsrc * NX + 2 * i + 1]], axis=1)
            cols = slice(2 * i * share, 2 * (i + 1) * share)
            cs_send[k, :, cols] = jnp.dot(mixp[0:half, :], right, preferred_element_type=jnp.float32).astype(jnp.bfloat16)
        copy = remote(cs_send.at[k], cs_recv.at[k], cs_ss.at[k], cs_rs.at[k], partner)
        copy.start()
        for i in range(NX // 2):
            right = jnp.concatenate([wo[zsrc * NX + 2 * i], wo[zsrc * NX + 2 * i + 1]], axis=1)
            cols = slice(2 * i * share, 2 * (i + 1) * share)
            own[k % 4, :, cols] = jnp.dot(mixp[half:, :], right, preferred_element_type=jnp.float32)
        return copy

    def rows_of(j):
        return slice(j * block, (j + 1) * block)

    def stage1(k):
        cs[k].wait_recv()
        slot = k % 4
        fs[k] = (own[slot, rows_of(2)] + cs_recv[k, rows_of(2)].astype(jnp.float32)).astype(jnp.bfloat16)
        first = remote(fs.at[k], fr.at[k], y_ss.at[0, k], y_rs.at[0, k], y_up)
        first.start()
        ms[k] = (own[slot, rows_of(3)] + cs_recv[k, rows_of(3)].astype(jnp.float32)).astype(jnp.bfloat16)
        minor = remote(ms.at[k], mr.at[k], y_ss.at[1, k], y_rs.at[1, k], y_down)
        minor.start()
        own[slot, 0 : 2 * block] = own[slot, 0 : 2 * block] + cs_recv[k, 0 : 2 * block].astype(jnp.float32)
        return first, minor

    def stage2(k):
        ys[k][0].wait_recv()
        js[k] = (own[k % 4, rows_of(1)] + fr[k].astype(jnp.float32)).astype(jnp.bfloat16)
        joined = remote(js.at[k], jr.at[k], y_ss.at[2, k], y_rs.at[2, k], y_up)
        joined.start()
        return joined

    def stage3(k):
        ys[k][1].wait_recv()
        jn[k].wait_recv()
        zsrc = lax.rem(z + CHUNKS[k][0], NZ)
        total = own[k % 4, rows_of(0)] + mr[k].astype(jnp.float32) + jr[k].astype(jnp.float32)
        result_ref[:, pl.ds(pl.multiple_of(zsrc * span, span), span)] = total.astype(jnp.bfloat16)

    cs, ys, jn = {}, {}, {}

    def stages(k):
        if k < NZ:
            cs[k] = stage0(k)
        if 1 <= k < NZ + 1:
            ys[k - 1] = stage1(k - 1)
        if 2 <= k < NZ + 2:
            jn[k - 2] = stage2(k - 2)
        if k >= 3:
            stage3(k - 3)

    def mixing():
        def conv(p):
            lax.fori_loop(p * tiles, (p + 1) * tiles, convolve, 0)
            send_mix(p)

        yield send_tail
        yield lambda: (feature_rows(blocks - 1), send_halo())
        for r in range(blocks - 2, 0, -1):
            yield lambda r=r: feature_rows(r)
            if r % 2 == 1:
                yield lambda p=r // 2 + 1: conv(p)
        yield lambda: (take_tail(), feature_rows(0))
        yield take_halo
        yield lambda: conv(0)
        yield order_rows

    queue, seen, projected, chunk = [], {(p, 0, 0) for p in range(4)}, 0, 0
    ready, tokens_in = set(), False
    waiting = [0, 1, 7, 2, 6, 3, 5, 4]
    for code in ORDER:
        if code == 64:
            og.begin()
            continue
        if code == 301:
            og.release()
            continue
        if code == 300:
            queue.pop(0)()
            continue
        if code >= 200:
            token_step(code - 200)
            tokens_in = code == 204
        else:
            part, dz, dx = code // 32, code % 32 // 4, code % 4
            (wg if part < 2 else og).arrive(part % 2, dz, dx)
            seen.add((part, dz, dx))
            if part >= 2 and all((p, dz, i) in seen for p in (2, 3) for i in range(NX)):
                ready.add(dz)
        while tokens_in and waiting:
            dz = waiting[0]
            twins = (dz, (NZ - dz) % NZ)
            if not all((p, d, i) in seen for p in (0, 1) for d in twins for i in range(2)):
                break
            waiting.pop(0)
            projected += 1
            for i in range(3):
                queue.append(lambda dz=dz, n=projected, i=i: project(dz, n == 1, n == NZ, i))
            if projected == NZ:
                queue.extend(mixing())
        if projected == NZ:
            while chunk < NZ and ready >= set(CHUNKS[chunk][1]):
                queue.append(lambda k=chunk: stages(k))
                chunk += 1
    for piece in queue:
        piece()
    for k in range(NZ, NZ + 3):
        stages(k)

    wg.finish()
    og.finish()
    flight["tail"].wait_send()
    flight["halo"].wait_send()
    for k in range(NZ):
        cs[k].wait_send()
        ys[k][0].wait_send()
        ys[k][1].wait_send()
        jn[k].wait_send()

    @pl.when(kind == 0)
    def _():
        for i in range(4):
            share_param(i).wait_send()

    @pl.when(kind == 1)
    def _():
        for i in range(3):
            swap_shard(i, ctx).wait_send()
            mix_copy(i).wait_send()
        for i in range(5):
            token_cross(i).wait_send()
        for way in (1, -1):
            for h in range(4):
                token_pass(h, way, y).wait_send()
            token_relay(way, from_side(way)).wait_send()


def per_device(tokens, qkv_weight, short_filter, long_filter, decay_rate, skip_gain, out_weight):
    tcount, depth = tokens.shape
    _, share, width = qkv_weight.shape
    taps = long_filter.shape[1]
    groups = long_filter.shape[0]
    span = NX * share
    block = tcount // (2 * NY)
    half = NY * block
    bf, f32 = jnp.bfloat16, jnp.float32
    dma = pltpu.SemaphoreType.DMA
    any_spec = pl.BlockSpec(memory_space=pl.ANY)
    vmem = pl.BlockSpec(memory_space=pltpu.VMEM)
    small = (NZ, block, span)
    return pl.pallas_call(
        kernel,
        out_shape=jax.ShapeDtypeStruct((block, depth), bf),
        in_specs=[any_spec, any_spec, vmem, vmem, vmem, vmem, any_spec],
        out_specs=vmem,
        scratch_shapes=[
            pltpu.VMEM(short_filter.shape, f32),
            pltpu.VMEM(long_filter.shape, f32),
            pltpu.VMEM((1, groups), f32),
            pltpu.VMEM((1, width), f32),
            pltpu.VMEM((tcount, depth), bf),
            pltpu.VMEM((depth, 3 * width), bf),
            pltpu.VMEM((NZ * NX, width, share), bf),
            pltpu.VMEM((8 + tcount, 3 * width), f32),
            pltpu.VMEM((tcount, width), f32),
            pltpu.VMEM((taps + tcount, width), bf),
            pltpu.VMEM((groups * taps, 2 * taps), bf),
            pltpu.VMEM((tcount, width), bf),
            pltpu.VMEM((tcount, width), bf),
            pltpu.VMEM((tcount, width), bf),
            pltpu.VMEM((4, half, span), f32),
            pltpu.VMEM((NZ, half, span), bf),
            pltpu.VMEM((NZ, half, span), bf),
            *[pltpu.VMEM(small, bf) for _ in range(6)],
            pltpu.VMEM((16, 3 * width), bf),
            pltpu.VMEM((16, 3 * width), bf),
            pltpu.VMEM((taps, width), bf),
            dma((9,)),
            dma((2, NZ, 2)),
            dma((2, NZ, 2)),
            dma((2, NZ, NX)),
            dma((2, NZ, NX)),
            dma((NZ,)),
            dma((NZ,)),
            dma((3, NZ)),
            dma((3, NZ)),
            dma((2,)),
            dma((2,)),
            dma((2, NZ, 2)),
            dma((2, NZ, 2)),
            dma((3,)),
            dma((3,)),
            dma((15,)),
            dma((15,)),
            dma((4,)),
            dma((4,)),
            dma((3,)),
            dma((3,)),
        ],
        compiler_params=pltpu.CompilerParams(
            collective_id=0, has_side_effects=True, vmem_limit_bytes=67043328
        ),
    )(
        tokens,
        qkv_weight,
        short_filter,
        long_filter,
        decay_rate[None, :],
        skip_gain[None, :],
        out_weight,
    )


def solution(mesh):
    in_specs = (
        P("ctx", None),
        P(None, "ctx", "tp"),
        P(None, None, "tp"),
        P("tp", None),
        P("tp"),
        P("tp"),
        P("tp", "ctx"),
    )
    out_specs = P(("ctx", "tp"), None)
    return jax.shard_map(
        per_device, mesh=mesh, in_specs=in_specs, out_specs=out_specs, check_vma=False
    )
```
